128 devices in a mesh: ctx: 32 (over x_hi, z, y), tp: 4 (over x_lo, core).
Axes of the slice: x: 4 (x_hi: 2, x_lo: 2; x = x_hi * 2 + x_lo), y: 4, z: 4, core: 2. Of those that a mesh axis runs over, the one named last changes fastest.
Arguments:
- qkv: bfloat16 [3, 8192, 4096], P(None, 'ctx', 'tp'), may hold values from -6 to 6
- filters: bfloat16 [256, 128], P('tp'), may hold values from -0.5 to 0.5
- w_out: bfloat16 [4096, 4096], P(None, 'tp'), may hold values from -0.09375 to 0.09375
- cotangent: bfloat16 [8192, 4096], P(('ctx', 'tp')), may hold values from -24 to 24
- doc_lens: int32 [64], replicated, may hold values from 1 to 384, 8192 in all
Outputs:
- grad_qkv: bfloat16 [3, 8192, 4096], P(None, 'ctx', 'tp')
- grad_filters: float32 [256, 128], P('tp')
- grad_w_out: float32 [4096, 4096], P('ctx', 'tp')
The draws below stay inside these ranges and needn't reach their ends.
All inputs are finite; a program needn't handle non-finite values.
Results may differ from the reference program's by a relative error of at most 0.005.
Values may be sent and summed in bfloat16 or wider, within the bound.
A program may use at most 128 MiB of HBM per device.

```python
import math
import jax
import jax.numpy as jnp
import numpy as np
from jax import lax

D = 4096
GROUP = 16
TAPS = 128
SPAN = 128
GROUPS = 256
TOKENS = 8192
NDOCS = 64
MOST = 384
N_CTX = 32


def raised(result, key, source, target, blocks, factor):
    owner, partner = [(jnp.arange(result.shape[axis_at]) // (result.shape[axis_at] // blocks)).reshape([-1 if axis == axis_at else 1 for axis in range(result.ndim)]) for axis_at in (source, target)]
    chosen = jax.random.permutation(key, blocks)[partner]
    strong = (owner == chosen) | (owner == (partner + blocks // 2) % blocks)
    return jnp.where(strong, factor * result, result)


def steps_of(stream_key, shape, split, low, largest):
    loudness, own = 1.0, jax.random.fold_in(stream_key, 6)
    for position, blocks in split:
        steps = jnp.exp(jax.random.uniform(jax.random.fold_in(own, position), (blocks,), jnp.float32, low / len(split), largest / len(split)))
        loudness = loudness * jnp.repeat(steps, shape[position] // blocks).reshape([-1 if axis == position else 1 for axis in range(len(shape))])
    return loudness


def profile(amount, total, bound, skew):
    loads = [(1 << 20) // math.isqrt(standing ** skew) + 1 for standing in range(2, amount + 1)]
    spare, given = total - bound - (amount - 1), [1] * (amount - 1)
    while spare > 0:
        free = [i for i in range(amount - 1) if given[i] < bound]
        whole, budget = sum([loads[i] for i in free]), spare
        for i in free:
            more = min(bound - given[i], max(1, budget * loads[i] // whole), spare)
            given[i] = given[i] + more
            spare = spare - more
    return np.array([bound] + given)


def uneven(stream_key, count, total, bound, skew):
    if count == 2:
        one = jax.random.randint(stream_key, (), max(1, total - bound), min(bound, total - 1) + 1)
        return jnp.stack([one, total - one])
    lengths = jnp.asarray(profile(count, total, bound, skew), jnp.int32)
    twos = (count - 1) // 2
    donor, sink = lengths[1:1 + 2 * twos:2], lengths[2:2 + 2 * twos:2]
    room = jnp.minimum(donor - 1, bound - sink)
    shifted = jax.random.randint(jax.random.fold_in(stream_key, 1), (twos,), 0, 1 << 20) % (room + 1)
    lengths = lengths.at[1:1 + 2 * twos:2].set(donor - shifted).at[2:2 + 2 * twos:2].set(sink + shifted)
    return lengths[jax.random.permutation(jax.random.fold_in(stream_key, 2), count)]


def centred(rng, extent, scale, reach, split=(), kind=jnp.bfloat16):
    entries = jax.random.normal(rng, extent, jnp.float32) * scale
    if len(split) > 0:
        entries = steps_of(rng, extent, split, -0.22, 0.18) * entries
    return jnp.clip(entries, min=-reach, max=reach).astype(kind)


def gaussian_with(own_key, extent, scale, reach, split, heavy, kind=jnp.bfloat16):
    result = scale * jax.random.normal(own_key, extent, jnp.float32)
    if split:
        result = result * steps_of(own_key, extent, split, -0.22, 0.18)
    return jnp.clip(raised(result, jax.random.fold_in(own_key, 3), *heavy), -reach, reach).astype(kind)


def setup_inputs(seed: int = 0) -> dict:
    streams_of = jax.random.split(jax.random.key(seed), 6)
    return {
        "qkv": centred(streams_of[0], (3, TOKENS, D), 1.0, 6.0, ((1, 32), (2, 4))),
        "filters": centred(streams_of[1], (GROUPS, TAPS), TAPS ** -0.5, 0.5, ((0, 4),)),
        "w_out": centred(streams_of[2], (D, D), D ** -0.5, 0.09375, ((1, 4),)),
        "cotangent": gaussian_with(streams_of[3], (TOKENS, D), 1.0, 24.0, ((0, 128),), (0, 1, 128, 5.5)),
        "doc_lens": uneven(streams_of[4], NDOCS, TOKENS, MOST, 1).astype(jnp.int32),
    }


def banded(filters):
    groups, tap_count = filters.shape
    width = 2 * tap_count
    blank = jnp.zeros((groups, 1), filters.dtype)
    tailing = jnp.zeros((groups, width - tap_count), filters.dtype)
    pattern = jnp.concatenate([blank, jnp.flip(filters, axis=1), tailing], axis=1)
    tiled = jnp.broadcast_to(pattern[:, None, :], (groups, tap_count, width + 1)).reshape(groups, tap_count * (width + 1))
    return tiled[:, :tap_count * width].reshape(groups, tap_count, width)

def diagonals(products):
    groups, tap_count, width = products.shape
    flattened = jnp.pad(products.reshape(groups, tap_count * width), ((0, 0), (0, tap_count)))
    sheared = flattened.reshape(groups, tap_count, width + 1)[:, :, 1:tap_count + 1]
    return jnp.flip(lax.optimization_barrier(jnp.sum(sheared, axis=1)), axis=1)

def doc_reach(positions, doc_lens):
    starts = (jnp.cumsum(doc_lens) - doc_lens).astype(jnp.int32)
    below = jnp.where(starts[None, :] <= positions[:, None], starts[None, :], 0)
    return (positions - lax.optimization_barrier(jnp.max(below, axis=1))).astype(jnp.int32)

def band_mask(doc_offset, tap_count, dtype):
    row_ids = lax.broadcasted_iota(jnp.int32, (tap_count, 2 * tap_count), 0)
    col_ids = lax.broadcasted_iota(jnp.int32, (tap_count, 2 * tap_count), 1)
    return (row_ids - col_ids + tap_count <= doc_offset[:, None]).astype(dtype)

def to_natural(array):
    leading = array.shape[:-2]
    chans = array.shape[-1]
    paired = array.reshape(leading + (N_CTX, 2, SPAN, chans))
    first_half = paired[..., 0, :, :]
    second_half = jnp.flip(paired[..., 1, :, :], axis=-3)
    return jnp.concatenate([first_half, second_half], axis=-3).reshape(leading + (TOKENS, chans))

def to_stored(array):
    leading = array.shape[:-2]
    chans = array.shape[-1]
    pieces = array.reshape(leading + (2 * N_CTX, SPAN, chans))
    first_half = pieces[..., :N_CTX, :, :]
    second_half = jnp.flip(pieces[..., N_CTX:, :, :], axis=-3)
    return jnp.stack([first_half, second_half], axis=-3).reshape(leading + (TOKENS, chans))

def reference(qkv, filters, w_out, cotangent, doc_lens):
    natural = to_natural(qkv)
    queries, keys, values = (natural[0], natural[1], natural[2])
    arriving = to_natural(cotangent)
    positions = jnp.arange(TOKENS, dtype=jnp.int32)
    doc_offset = doc_reach(positions, doc_lens)
    hidden = (keys.astype(jnp.float32) * values.astype(jnp.float32)).astype(jnp.bfloat16)
    grad_y = jnp.dot(arriving, w_out, preferred_element_type=jnp.float32)
    grad_c = (queries.astype(jnp.float32) * grad_y).astype(jnp.bfloat16)
    kernel_base = banded(filters.astype(jnp.float32))
    padded_h = jnp.concatenate([jnp.zeros((TAPS, D), jnp.bfloat16), hidden], axis=0)
    exact = lax.Precision.HIGHEST

    def one_block(block_index):
        start = (block_index * TAPS).astype(jnp.int32)
        window = lax.dynamic_slice_in_dim(padded_h, start, 2 * TAPS, 0).astype(jnp.float32).reshape(2 * TAPS, GROUPS, GROUP)
        rows_grad = lax.dynamic_slice_in_dim(grad_c, start, TAPS, 0).astype(jnp.float32).reshape(TAPS, GROUPS, GROUP)
        keep = band_mask(lax.dynamic_slice_in_dim(doc_offset, start, TAPS, 0), TAPS, jnp.float32)
        kernel = kernel_base * keep[None]
        conv_rows = jnp.einsum('gij,jgc->igc', kernel, window, precision=exact).reshape(TAPS, D)
        spread = jnp.einsum('gij,igc->jgc', kernel, rows_grad, precision=exact).reshape(2 * TAPS, D)
        products = jnp.einsum('igc,jgc->gij', rows_grad, window, precision=exact)
        return (conv_rows, spread[:TAPS], spread[TAPS:], diagonals(products * keep[None]))
    conv_blocks, spill_rows, own_rows, filter_parts = lax.map(one_block, jnp.arange(TOKENS // TAPS, dtype=jnp.int32))
    conv_out = conv_blocks.reshape(TOKENS, D)
    following = jnp.concatenate([spill_rows[1:], jnp.zeros((1, TAPS, D), jnp.float32)], axis=0)
    grad_h = (own_rows + following).reshape(TOKENS, D)
    grad_q = (grad_y * conv_out).astype(jnp.bfloat16)
    grad_k = (grad_h * values.astype(jnp.float32)).astype(jnp.bfloat16)
    grad_v = (grad_h * keys.astype(jnp.float32)).astype(jnp.bfloat16)
    grad_qkv = to_stored(jnp.stack([grad_q, grad_k, grad_v]))
    grad_scale = 1.0 / math.sqrt(TOKENS)
    grad_filters = lax.optimization_barrier(jnp.sum(filter_parts, axis=0)) * grad_scale
    gated = (queries.astype(jnp.float32) * conv_out).astype(jnp.bfloat16)
    grad_w = jnp.dot(arriving.T, gated, preferred_element_type=jnp.float32) * grad_scale
    return (grad_qkv, grad_filters, grad_w)
```

```python
import functools
import math

import jax
import jax.numpy as jnp
from jax import lax
from jax.experimental import pallas as pl
from jax.experimental.pallas import tpu as pltpu
from jax.sharding import PartitionSpec as P

F32 = jnp.float32
BF16 = jnp.bfloat16
MESH = pl.DeviceIdType.MESH
BIG = 64 * 1024 * 1024 - 65536
SPAN = 128
LANES = 128


def doc_starts_row(doc_ref, pos):
    def step(d, carry):
        start, best = carry
        best = jnp.where(pos >= start, start, best)
        return start + doc_ref[d], best

    return lax.fori_loop(0, doc_ref.shape[0], step, (jnp.int32(0), jnp.zeros_like(pos)))[1]


def as_column(row):
    return jnp.broadcast_to(row.astype(F32), (LANES, LANES)).T.astype(jnp.int32)


def sheared(padded, base_ref):
    groups = padded.shape[0]
    for r in range(8):
        turned = padded if r == 0 else pltpu.roll(padded, r, 1)
        for n in range(2):
            base_ref[n, pl.ds(r, groups, stride=8), :] = turned[:, n * LANES : (n + 1) * LANES]


def toeplitz(base_ref, out_ref):
    def one(g, carry):
        rows = pl.ds(pl.multiple_of(g * 8, 8), 8)
        slab = jnp.concatenate([base_ref[0, rows, :], base_ref[1, rows, :]], axis=1)
        for q in range(0, 16, 2):
            low = slab if q == 0 else pltpu.roll(slab, 8 * q, 1)
            high = pltpu.roll(slab, 8 * q + 8, 1)
            out_ref[g, 8 * q : 8 * q + 16, :] = jnp.concatenate([low, high], axis=0).astype(BF16)
        return carry

    lax.fori_loop(0, out_ref.shape[0], one, 0)


def flipped(filters):
    row = lax.broadcasted_iota(jnp.int32, (LANES, LANES), 0)
    col = lax.broadcasted_iota(jnp.int32, (LANES, LANES), 1)
    anti = (row + col == LANES - 1).astype(F32).astype(BF16)
    return jnp.dot(filters, anti, preferred_element_type=F32)


def block_position(slot, rank, count):
    return (rank if slot == 0 else 2 * count - 1 - rank) * SPAN


def window_mask(doc_ref, start):
    lane = lax.broadcasted_iota(jnp.int32, (1, LANES), 1)
    begins = as_column(doc_starts_row(doc_ref, lane + start))
    begins = jnp.concatenate([begins, begins], axis=1)
    col = lax.broadcasted_iota(jnp.int32, (SPAN, 2 * SPAN), 1) + (start - SPAN)
    return (col >= begins).astype(jnp.int32)


def spread_mask(doc_ref, start, next_start):
    lane = lax.broadcasted_iota(jnp.int32, (1, LANES), 1)
    begins = jnp.concatenate(
        [doc_starts_row(doc_ref, lane + start), doc_starts_row(doc_ref, lane + next_start)], axis=1
    )
    row = lax.broadcasted_iota(jnp.int32, (SPAN, 2 * SPAN), 0) + start
    return (row >= jnp.broadcast_to(begins, (SPAN, 2 * SPAN))).astype(jnp.int32)


def conv_kernel(count, doc_ref, filt_ref, qkv_ref, prev_ref, c_ref, yt_ref, base, toep, mask, win):
    rank = lax.axis_index("ctx")
    flip = flipped(filt_ref[...])
    sheared(pltpu.roll(jnp.concatenate([flip, jnp.zeros_like(flip)], axis=1), 1, 1), base)
    toeplitz(base, toep)
    for slot in range(2):
        mask[slot] = (
            window_mask(doc_ref, block_position(slot, rank, count)).astype(F32).astype(BF16)
        )
        win[slot, :SPAN] = prev_ref[slot]
        rows = slice(slot * SPAN, (slot + 1) * SPAN)
        win[slot, SPAN:] = (qkv_ref[1, rows].astype(F32) * qkv_ref[2, rows].astype(F32)).astype(
            BF16
        )
    owner = lax.broadcasted_iota(jnp.int32, (SPAN, LANES), 1) // 16
    tiles = c_ref.shape[1] // LANES

    def tile(n, carry):
        slot, t = n // tiles, n % tiles
        cols = pl.ds(pl.multiple_of(t * LANES, LANES), LANES)
        rows = pl.ds(pl.multiple_of(slot * SPAN, SPAN), SPAN)
        window = win[slot, :, cols]
        keep = mask[slot]
        total = jnp.zeros((SPAN, LANES), F32)
        for u in range(8):
            part = jnp.dot(toep[t * 8 + u] * keep, window, preferred_element_type=F32)
            total = jnp.where(owner == u, part, total)
        c_ref[rows, cols] = total
        gated = (qkv_ref[0, rows, cols].astype(F32) * total).astype(BF16).astype(F32)
        yt_ref[cols, rows] = gated.T.astype(BF16)
        return carry

    lax.fori_loop(0, 2 * tiles, tile, 0)


def conv_call(doc_lens, filters, qkv, prev, count):
    groups = filters.shape[0]
    width = qkv.shape[2]
    return pl.pallas_call(
        functools.partial(conv_kernel, count),
        out_shape=(
            jax.ShapeDtypeStruct((2 * SPAN, width), F32),
            jax.ShapeDtypeStruct((width, 2 * SPAN), BF16),
        ),
        in_specs=[pl.BlockSpec(memory_space=pltpu.SMEM)]
        + [pl.BlockSpec(memory_space=pltpu.VMEM)] * 3,
        out_specs=(pl.BlockSpec(memory_space=pltpu.VMEM),) * 2,
        scratch_shapes=[
            pltpu.VMEM((2, 8 * groups, SPAN), F32),
            pltpu.VMEM((groups, SPAN, 2 * SPAN), BF16),
            pltpu.VMEM((2, SPAN, 2 * SPAN), BF16),
            pltpu.VMEM((2, 2 * SPAN, width), BF16),
        ],
        compiler_params=pltpu.CompilerParams(vmem_limit_bytes=40 * 1024 * 1024),
        name="conv",
    )(doc_lens, filters, qkv, prev)


def back_kernel(
    count,
    doc_ref,
    filt_ref,
    qkv_ref,
    prev_ref,
    dc_ref,
    dcn_ref,
    gq_ref,
    out_ref,
    gf_ref,
    base,
    toep,
    spread,
    keep,
    win,
    dwin,
    diag,
):
    rank = lax.axis_index("ctx")
    filt = filt_ref[...].astype(F32)
    sheared(jnp.concatenate([filt, jnp.zeros_like(filt)], axis=1), base)
    toeplitz(base, toep)
    out_ref[0] = gq_ref[...]
    for slot in range(2):
        start = block_position(slot, rank, count)
        follow = (rank + 1) * SPAN if slot == 0 else (2 * count - rank) * SPAN
        keep[slot] = window_mask(doc_ref, start).astype(F32)
        spread[slot] = spread_mask(doc_ref, start, follow).astype(F32).astype(BF16)
        rows = slice(slot * SPAN, (slot + 1) * SPAN)
        win[slot, :SPAN] = prev_ref[slot]
        win[slot, SPAN:] = (qkv_ref[1, rows].astype(F32) * qkv_ref[2, rows].astype(F32)).astype(
            BF16
        )
        dwin[slot, :SPAN] = dc_ref[rows]
        dwin[slot, SPAN:] = dcn_ref[slot]
    owner = lax.broadcasted_iota(jnp.int32, (SPAN, LANES), 1) // 16
    tiles = dc_ref.shape[1] // LANES

    def tile(n, carry):
        slot, t = n // tiles, n % tiles
        cols = pl.ds(pl.multiple_of(t * LANES, LANES), LANES)
        rows = pl.ds(pl.multiple_of(slot * SPAN, SPAN), SPAN)
        window = dwin[slot, :, cols]
        mask = spread[slot]
        total = jnp.zeros((SPAN, LANES), F32)
        for u in range(8):
            part = jnp.dot(toep[t * 8 + u] * mask, window, preferred_element_type=F32)
            total = jnp.where(owner == u, part, total)
        out_ref[1, rows, cols] = (total * qkv_ref[2, rows, cols].astype(F32)).astype(BF16)
        out_ref[2, rows, cols] = (total * qkv_ref[1, rows, cols].astype(F32)).astype(BF16)
        return carry

    lax.fori_loop(0, 2 * tiles, tile, 0)

    def taps(t, carry):
        cols = pl.ds(pl.multiple_of(t * LANES, LANES), LANES)
        for u in range(8):
            both = None
            for slot in range(2):
                grad = dwin[slot, :SPAN, cols].astype(F32)
                grad = jnp.where(owner == u, grad, 0.0).astype(BF16)
                prod = lax.dot_general(
                    grad, win[slot, :, cols], (((1,), (1,)), ((), ())), preferred_element_type=F32
                )
                prod = prod * keep[slot]
                both = prod if both is None else both + prod
            slabs = [both[8 * q : 8 * q + 8] for q in range(16)]
            while len(slabs) > 1:
                half = len(slabs) // 2
                slabs = [
                    slabs[q] + pltpu.roll(slabs[q + half], 2 * SPAN - 8 * half, 1)
                    for q in range(half)
                ]
            rows = pl.ds(pl.multiple_of(t * 64 + u * 8, 8), 8)
            diag[0, rows, :] = slabs[0][:, :LANES]
            diag[1, rows, :] = slabs[0][:, LANES:]
        return carry

    lax.fori_loop(0, tiles, taps, 0)
    groups = gf_ref.shape[0]
    total = None
    for r in range(8):
        row = jnp.concatenate([diag[n, pl.ds(r, groups, stride=8), :] for n in range(2)], axis=1)
        total = row if r == 0 else total + pltpu.roll(row, 2 * SPAN - r, 1)
    gf_ref[...] = pltpu.roll(total, 2 * SPAN - 1, 1)[:, :LANES]


def back_call(doc_lens, filters, qkv, prev, dc, dcn, gq, count):
    groups = filters.shape[0]
    width = qkv.shape[2]
    return pl.pallas_call(
        functools.partial(back_kernel, count),
        out_shape=(
            jax.ShapeDtypeStruct(qkv.shape, BF16),
            jax.ShapeDtypeStruct((groups, LANES), F32),
        ),
        in_specs=[pl.BlockSpec(memory_space=pltpu.SMEM)]
        + [pl.BlockSpec(memory_space=pltpu.VMEM)] * 6,
        out_specs=(pl.BlockSpec(memory_space=pltpu.VMEM),) * 2,
        scratch_shapes=[
            pltpu.VMEM((2, 8 * groups, SPAN), F32),
            pltpu.VMEM((groups, SPAN, 2 * SPAN), BF16),
            pltpu.VMEM((2, SPAN, 2 * SPAN), BF16),
            pltpu.VMEM((2, SPAN, 2 * SPAN), F32),
            pltpu.VMEM((2, 2 * SPAN, width), BF16),
            pltpu.VMEM((2, 2 * SPAN, width), BF16),
            pltpu.VMEM((2, 8 * groups, SPAN), F32),
        ],
        compiler_params=pltpu.CompilerParams(vmem_limit_bytes=40 * 1024 * 1024),
        name="back",
    )(doc_lens, filters, qkv, prev, dc, dcn, gq)


def project_kernel(
    scale,
    cot_ref,
    yt_ref,
    w_ref,
    qkv_ref,
    c_ref,
    gw_ref,
    dc_ref,
    gq_ref,
    full,
    w_v,
    q_v,
    part,
    relay1,
    done1,
    red,
    relay2,
    done2,
    away,
    kept,
    far,
    load_sem,
    cot_send,
    cot_recv,
    send1,
    recv1,
    send2,
    recv2,
    far_send,
    far_recv,
):
    ctx = lax.axis_index("ctx")
    tp = lax.axis_index("tp")
    my_y = ctx % 4
    my_z = (ctx // 4) % 4
    my_x = ctx // 16
    place = (my_y, my_z)
    stride = (1, 4)
    rows_local = cot_ref.shape[0]

    def around(axis, step):
        return ctx + stride[axis] * ((place[axis] + step) % 4 - place[axis])

    across = ctx + 16 - 32 * my_x
    core = tp + 1 - 2 * (tp % 2)
    beside = tp + 2 - 4 * (tp // 2)

    barrier = pltpu.get_barrier_semaphore()
    for axis in range(2):
        for step in (1, 3):
            pl.semaphore_signal(
                barrier, inc=1, device_id=(around(axis, step), tp), device_id_type=MESH
            )
    pl.semaphore_signal(barrier, inc=1, device_id=(across, tp), device_id_type=MESH)
    pl.semaphore_signal(barrier, inc=1, device_id=(ctx, core), device_id_type=MESH)
    pl.semaphore_signal(barrier, inc=1, device_id=(ctx, beside), device_id_type=MESH)
    load_w = pltpu.make_async_copy(w_ref, w_v, load_sem.at[0])
    load_q = pltpu.make_async_copy(qkv_ref.at[0], q_v, load_sem.at[1])
    pl.semaphore_wait(barrier, 7)

    half_cols = cot_ref.shape[1] // 2
    col0 = [
        pl.multiple_of((1 - my_x) * half_cols, half_cols),
        pl.multiple_of(my_x * half_cols, half_cols),
    ]

    def cot_copy(k, n, src, owner, target):
        rows = pl.ds(pl.multiple_of(owner * rows_local, rows_local), rows_local)
        cols = pl.ds(col0[k], half_cols)
        return pltpu.make_async_remote_copy(
            src_ref=cot_ref.at[:, cols] if src is None else full.at[rows, cols],
            dst_ref=full.at[rows, cols],
            send_sem=cot_send.at[k, n],
            recv_sem=cot_recv.at[k, n],
            device_id=(ctx, target),
            device_id_type=MESH,
        )

    side = [cot_copy(k, 0, None, tp, beside) for k in range(2)]
    near = [cot_copy(k, 1, None, tp, core) for k in range(2)]
    pass_on = [cot_copy(k, 2, full, beside, core) for k in range(2)]
    for k in range(2):
        side[k].start()
        near[k].start()
    load_w.start()
    load_q.start()
    full[pl.ds(pl.multiple_of(tp * rows_local, rows_local), rows_local), :] = cot_ref[...]

    def gather(k):
        side[k].wait_recv()
        pass_on[k].start()
        near[k].wait_recv()
        pass_on[k].wait_recv()

    def partial(k):
        def block(i, carry):
            tokens = full[:, pl.ds(pl.multiple_of(col0[k] + i * 256, 256), 256)]

            def some(m, inner):
                rows = pl.ds(pl.multiple_of(m * 256, 256), 256)
                out = jnp.dot(yt_ref[rows, :], tokens, preferred_element_type=F32).astype(BF16)
                part[k, i // 2, (i % 2) * 2, rows, :] = out[:, :LANES]
                part[k, i // 2, (i % 2) * 2 + 1, rows, :] = out[:, LANES:]
                return inner

            return lax.fori_loop(0, 4, some, carry)

        lax.fori_loop(0, 8, block, 0)

    def quarter(axis, half):
        first = axis * 512 + half * 256
        return slice(first, first + 256)

    def piece1(axis, k, j, half):
        if axis == 0:
            return part.at[k, :, j, quarter(axis, half)]
        return part.at[k, j, :, quarter(axis, half)]

    def piece2(axis, k, j, half):
        return red.at[axis, k, j, pl.ds(half * 256, 256)]

    def ring(stage, axis, k):
        ring_axis = axis if stage == 1 else 1 - axis
        m = place[ring_axis]
        up, down = around(ring_axis, 1), around(ring_axis, 3)
        piece = piece1 if stage == 1 else piece2
        relays = relay1 if stage == 1 else relay2
        done = done1 if stage == 1 else done2
        send, recv = (send1, recv1) if stage == 1 else (send2, recv2)
        nxt, prv, opp = (m + 1) % 4, (m + 3) % 4, (m + 2) % 4
        table = [
            (piece(axis, k, opp, 0), relays.at[axis, k, 0], up),
            (piece(axis, k, opp, 1), relays.at[axis, k, 1], down),
            (piece(axis, k, nxt, 1), done.at[axis, k, 0], up),
            (piece(axis, k, prv, 0), done.at[axis, k, 1], down),
            (piece(axis, k, nxt, 0), done.at[axis, k, 2], up),
            (piece(axis, k, prv, 1), done.at[axis, k, 3], down),
        ]
        copies = [
            pltpu.make_async_remote_copy(
                src_ref=src,
                dst_ref=dst,
                send_sem=send.at[axis, k, n],
                recv_sem=recv.at[axis, k, n],
                device_id=(target, tp),
                device_id_type=MESH,
            )
            for n, (src, dst, target) in enumerate(table)
        ]

        def start():
            for n in range(4):
                copies[n].start()

        def forward():
            for n in range(2):
                copies[n].wait_recv()
                mine = piece(axis, k, nxt if n == 0 else prv, n)
                mine[...] = (mine[...].astype(F32) + relays[axis, k, n].astype(F32)).astype(BF16)
                copies[4 + n].start()

        def finish(half):
            copies[3 if half == 0 else 2].wait_recv()
            copies[4 if half == 0 else 5].wait_recv()
            total = piece(axis, k, m, half)[...].astype(F32)
            total = total + done[axis, k, 1 if half == 0 else 0].astype(F32)
            return total + done[axis, k, 2 if half == 0 else 3].astype(F32)

        return start, forward, finish, copies

    first = [[ring(1, axis, k) for axis in range(2)] for k in range(2)]
    second = [[ring(2, axis, k) for axis in range(2)] for k in range(2)]

    for k in range(2):
        gather(k)
        partial(k)
        for axis in range(2):
            first[k][axis][0]()

    load_w.wait()
    load_q.wait()

    def project(n, carry):
        cols = pl.ds(pl.multiple_of(n * 256, 256), 256)
        dy = jnp.dot(full[...], w_v[:, cols], preferred_element_type=F32)
        dc_ref[:, cols] = (q_v[:, cols].astype(F32) * dy).astype(BF16)
        gq_ref[:, cols] = (dy * c_ref[:, cols]).astype(BF16)
        return carry

    lax.fori_loop(0, 4, project, 0)

    for k in range(2):
        for axis in range(2):
            first[k][axis][1]()
    for k in range(2):
        for axis in range(2):
            for half in range(2):
                red[axis, k, :, half * 256 : half * 256 + 256, :] = first[k][axis][2](half).astype(
                    BF16
                )
            second[k][axis][0]()
    for k in range(2):
        for axis in range(2):
            second[k][axis][1]()
    for k in range(2):
        for axis in range(2):
            for half in range(2):
                total = second[k][axis][2](half)
                if k == 0:
                    away[quarter(axis, half)] = total.astype(BF16)
                else:
                    kept[quarter(axis, half)] = total
        if k == 0:
            over = pltpu.make_async_remote_copy(
                src_ref=away,
                dst_ref=far,
                send_sem=far_send,
                recv_sem=far_recv,
                device_id=(across, tp),
                device_id_type=MESH,
            )
            over.start()
    over.wait_recv()
    for n in range(8):
        rows = slice(n * LANES, (n + 1) * LANES)
        gw_ref[:, rows] = ((kept[rows] + far[rows].astype(F32)) * scale).T
    over.wait_send()
    for k in range(2):
        side[k].wait_send()
        near[k].wait_send()
        pass_on[k].wait_send()
        for axis in range(2):
            for copy in first[k][axis][3] + second[k][axis][3]:
                copy.wait_send()


def project_call(cot, yt, w_out, qkv, c, scale):
    rows_local, feats = cot.shape
    width = w_out.shape[1]
    tokens = qkv.shape[1]
    vm = pl.BlockSpec(memory_space=pltpu.VMEM)
    hb = pl.BlockSpec(memory_space=pl.ANY)
    return pl.pallas_call(
        functools.partial(project_kernel, scale),
        out_shape=(
            jax.ShapeDtypeStruct((feats // 32, width), F32),
            jax.ShapeDtypeStruct((tokens, width), BF16),
            jax.ShapeDtypeStruct((tokens, width), BF16),
        ),
        in_specs=[vm, vm, hb, hb, vm],
        out_specs=(vm, vm, vm),
        scratch_shapes=[
            pltpu.VMEM((tokens, feats), BF16),
            pltpu.VMEM((feats, width), BF16),
            pltpu.VMEM((tokens, width), BF16),
            pltpu.VMEM((2, 4, 4, width, LANES), BF16),
            pltpu.VMEM((2, 2, 2, 4, 256, LANES), BF16),
            pltpu.VMEM((2, 2, 4, 4, 256, LANES), BF16),
            pltpu.VMEM((2, 2, 4, 512, LANES), BF16),
            pltpu.VMEM((2, 2, 2, 256, LANES), BF16),
            pltpu.VMEM((2, 2, 4, 256, LANES), BF16),
            pltpu.VMEM((width, LANES), BF16),
            pltpu.VMEM((width, LANES), F32),
            pltpu.VMEM((width, LANES), BF16),
            pltpu.SemaphoreType.DMA((2,)),
            pltpu.SemaphoreType.DMA((2, 3)),
            pltpu.SemaphoreType.DMA((2, 3)),
            pltpu.SemaphoreType.DMA((2, 2, 6)),
            pltpu.SemaphoreType.DMA((2, 2, 6)),
            pltpu.SemaphoreType.DMA((2, 2, 6)),
            pltpu.SemaphoreType.DMA((2, 2, 6)),
            pltpu.SemaphoreType.DMA,
            pltpu.SemaphoreType.DMA,
        ],
        compiler_params=pltpu.CompilerParams(
            vmem_limit_bytes=60 * 1024 * 1024, collective_id=0, has_side_effects=True
        ),
        name="project",
    )(cot, yt, w_out, qkv, c)


def neighbours(low, high, count):
    ahead = lax.ppermute(low, "ctx", [(i, i + 1) for i in range(count - 1)])
    behind = lax.ppermute(high, "ctx", [(i + 1, i) for i in range(count - 1)])
    return ahead, behind


def local(qkv, filters, w_out, cotangent, doc_lens):
    count = lax.axis_size("ctx")
    last = lax.axis_index("ctx") == count - 1
    tokens = qkv.shape[1] * count
    scale = 1.0 / math.sqrt(tokens)
    hidden = (qkv[1].astype(F32) * qkv[2].astype(F32)).astype(BF16)
    before, after = neighbours(hidden[:SPAN], hidden[SPAN:], count)
    prev = jnp.stack([before, jnp.where(last, hidden[:SPAN], after)])
    conv, gated = conv_call(doc_lens, filters, qkv, prev, count)
    grad_w, grad_c, grad_q = project_call(cotangent, gated, w_out, qkv, conv, scale)
    before, after = neighbours(grad_c[SPAN:], grad_c[:SPAN], count)
    follow = jnp.stack([jnp.where(last, grad_c[SPAN:], after), before])
    grad_qkv, taps = back_call(doc_lens, filters, qkv, prev, grad_c, follow, grad_q, count)
    taps = lax.psum(taps, "ctx")
    return grad_qkv, jnp.flip(taps, axis=1) * scale, grad_w


def solution(mesh):
    return jax.shard_map(
        local,
        mesh=mesh,
        in_specs=(P(None, "ctx", "tp"), P("tp", None), P(None, "tp"), P(("ctx", "tp"), None), P()),
        out_specs=(P(None, "ctx", "tp"), P("tp", None), P("ctx", "tp")),
        check_vma=False,
    )
```

```python
import functools
import math

import jax
import jax.numpy as jnp
from jax import lax
from jax.experimental import pallas as pl
from jax.experimental.pallas import tpu as pltpu
from jax.sharding import PartitionSpec as P

F32 = jnp.float32
BF16 = jnp.bfloat16
MESH = pl.DeviceIdType.MESH
BIG = 64 * 1024 * 1024 - 65536
SPAN = 128
LANES = 128


def doc_starts_row(doc_ref, pos):
    def step(d, carry):
        start, best = carry
        best = jnp.where(pos >= start, start, best)
        return start + doc_ref[d], best

    return lax.fori_loop(0, doc_ref.shape[0], step, (jnp.int32(0), jnp.zeros_like(pos)))[1]


def as_column(row):
    return jnp.broadcast_to(row.astype(F32), (LANES, LANES)).T.astype(jnp.int32)


def sheared(padded, base_ref):
    groups = padded.shape[0]
    for r in range(8):
        turned = padded if r == 0 else pltpu.roll(padded, r, 1)
        for n in range(2):
            base_ref[n, pl.ds(r, groups, stride=8), :] = turned[:, n * LANES : (n + 1) * LANES]


def toeplitz(base_ref, out_ref):
    def one(g, carry):
        rows = pl.ds(pl.multiple_of(g * 8, 8), 8)
        slab = jnp.concatenate([base_ref[0, rows, :], base_ref[1, rows, :]], axis=1)
        for q in range(0, 16, 2):
            low = slab if q == 0 else pltpu.roll(slab, 8 * q, 1)
            high = pltpu.roll(slab, 8 * q + 8, 1)
            out_ref[g, 8 * q : 8 * q + 16, :] = jnp.concatenate([low, high], axis=0).astype(BF16)
        return carry

    lax.fori_loop(0, out_ref.shape[0], one, 0)


def flipped(filters):
    row = lax.broadcasted_iota(jnp.int32, (LANES, LANES), 0)
    col = lax.broadcasted_iota(jnp.int32, (LANES, LANES), 1)
    anti = (row + col == LANES - 1).astype(F32).astype(BF16)
    return jnp.dot(filters, anti, preferred_element_type=F32)


def block_position(slot, rank, count):
    return (rank if slot == 0 else 2 * count - 1 - rank) * SPAN


def window_mask(doc_ref, start):
    lane = lax.broadcasted_iota(jnp.int32, (1, LANES), 1)
    begins = as_column(doc_starts_row(doc_ref, lane + start))
    begins = jnp.concatenate([begins, begins], axis=1)
    col = lax.broadcasted_iota(jnp.int32, (SPAN, 2 * SPAN), 1) + (start - SPAN)
    return (col >= begins).astype(jnp.int32)


def spread_mask(doc_ref, start, next_start):
    lane = lax.broadcasted_iota(jnp.int32, (1, LANES), 1)
    begins = jnp.concatenate(
        [doc_starts_row(doc_ref, lane + start), doc_starts_row(doc_ref, lane + next_start)], axis=1
    )
    row = lax.broadcasted_iota(jnp.int32, (SPAN, 2 * SPAN), 0) + start
    return (row >= jnp.broadcast_to(begins, (SPAN, 2 * SPAN))).astype(jnp.int32)


def conv_kernel(count, doc_ref, filt_ref, qkv_ref, prev_ref, c_ref, yt_ref, base, toep, mask, win):
    rank = lax.axis_index("ctx")
    flip = flipped(filt_ref[...])
    sheared(pltpu.roll(jnp.concatenate([flip, jnp.zeros_like(flip)], axis=1), 1, 1), base)
    toeplitz(base, toep)
    for slot in range(2):
        mask[slot] = (
            window_mask(doc_ref, block_position(slot, rank, count)).astype(F32).astype(BF16)
        )
        win[slot, :SPAN] = prev_ref[slot]
        rows = slice(slot * SPAN, (slot + 1) * SPAN)
        win[slot, SPAN:] = (qkv_ref[1, rows].astype(F32) * qkv_ref[2, rows].astype(F32)).astype(
            BF16
        )
    owner = lax.broadcasted_iota(jnp.int32, (SPAN, LANES), 1) // 16
    tiles = c_ref.shape[1] // LANES

    def tile(n, carry):
        slot, t = n // tiles, n % tiles
        cols = pl.ds(pl.multiple_of(t * LANES, LANES), LANES)
        rows = pl.ds(pl.multiple_of(slot * SPAN, SPAN), SPAN)
        window = win[slot, :, cols]
        keep = mask[slot]
        total = jnp.zeros((SPAN, LANES), F32)
        for u in range(8):
            part = jnp.dot(toep[t * 8 + u] * keep, window, preferred_element_type=F32)
            total = jnp.where(owner == u, part, total)
        c_ref[rows, cols] = total
        gated = (qkv_ref[0, rows, cols].astype(F32) * total).astype(BF16).astype(F32)
        yt_ref[cols, rows] = gated.T.astype(BF16)
        return carry

    lax.fori_loop(0, 2 * tiles, tile, 0)


def conv_call(doc_lens, filters, qkv, prev, count):
    groups = filters.shape[0]
    width = qkv.shape[2]
    return pl.pallas_call(
        functools.partial(conv_kernel, count),
        out_shape=(
            jax.ShapeDtypeStruct((2 * SPAN, width), F32),
            jax.ShapeDtypeStruct((width, 2 * SPAN), BF16),
        ),
        in_specs=[pl.BlockSpec(memory_space=pltpu.SMEM)]
        + [pl.BlockSpec(memory_space=pltpu.VMEM)] * 3,
        out_specs=(pl.BlockSpec(memory_space=pltpu.VMEM),) * 2,
        scratch_shapes=[
            pltpu.VMEM((2, 8 * groups, SPAN), F32),
            pltpu.VMEM((groups, SPAN, 2 * SPAN), BF16),
            pltpu.VMEM((2, SPAN, 2 * SPAN), BF16),
            pltpu.VMEM((2, 2 * SPAN, width), BF16),
        ],
        compiler_params=pltpu.CompilerParams(vmem_limit_bytes=40 * 1024 * 1024),
        name="conv",
    )(doc_lens, filters, qkv, prev)


def back_kernel(
    count,
    doc_ref,
    filt_ref,
    qkv_ref,
    prev_ref,
    dc_ref,
    dcn_ref,
    gq_ref,
    out_ref,
    gf_ref,
    base,
    toep,
    spread,
    keep,
    win,
    dwin,
    diag,
    tap_y,
    tap_z,
    tap_x,
    tap_send,
    tap_recv,
):
    rank = lax.axis_index("ctx")
    tp = lax.axis_index("tp")
    place = (rank % 4, (rank // 4) % 4)
    across = rank + 16 - 32 * (rank // 16)

    def around(axis, step):
        return rank + (1, 4)[axis] * ((place[axis] + step) % 4 - place[axis])

    partners = [[around(axis, step) for step in (1, 2, 3)] for axis in range(2)] + [[across]]
    barrier = pltpu.get_barrier_semaphore()
    for targets in partners:
        for target in targets:
            pl.semaphore_signal(barrier, inc=1, device_id=(target, tp), device_id_type=MESH)
    pl.semaphore_wait(barrier, 7)
    filt = filt_ref[...].astype(F32)
    sheared(jnp.concatenate([filt, jnp.zeros_like(filt)], axis=1), base)
    toeplitz(base, toep)
    out_ref[0] = gq_ref[...]
    for slot in range(2):
        start = block_position(slot, rank, count)
        follow = (rank + 1) * SPAN if slot == 0 else (2 * count - rank) * SPAN
        keep[slot] = window_mask(doc_ref, start).astype(F32)
        spread[slot] = spread_mask(doc_ref, start, follow).astype(F32).astype(BF16)
        rows = slice(slot * SPAN, (slot + 1) * SPAN)
        win[slot, :SPAN] = prev_ref[slot]
        win[slot, SPAN:] = (qkv_ref[1, rows].astype(F32) * qkv_ref[2, rows].astype(F32)).astype(
            BF16
        )
        dwin[slot, :SPAN] = dc_ref[rows]
        dwin[slot, SPAN:] = dcn_ref[slot]
    owner = lax.broadcasted_iota(jnp.int32, (SPAN, LANES), 1) // 16
    tiles = dc_ref.shape[1] // LANES

    def tile(n, carry):
        slot, t = n // tiles, n % tiles
        cols = pl.ds(pl.multiple_of(t * LANES, LANES), LANES)
        rows = pl.ds(pl.multiple_of(slot * SPAN, SPAN), SPAN)
        window = dwin[slot, :, cols]
        mask = spread[slot]
        total = jnp.zeros((SPAN, LANES), F32)
        for u in range(8):
            part = jnp.dot(toep[t * 8 + u] * mask, window, preferred_element_type=F32)
            total = jnp.where(owner == u, part, total)
        out_ref[1, rows, cols] = (total * qkv_ref[2, rows, cols].astype(F32)).astype(BF16)
        out_ref[2, rows, cols] = (total * qkv_ref[1, rows, cols].astype(F32)).astype(BF16)
        return carry

    lax.fori_loop(0, 2 * tiles, tile, 0)

    def taps(t, carry):
        cols = pl.ds(pl.multiple_of(t * LANES, LANES), LANES)
        for u in range(8):
            both = None
            for slot in range(2):
                grad = dwin[slot, :SPAN, cols].astype(F32)
                grad = jnp.where(owner == u, grad, 0.0).astype(BF16)
                prod = lax.dot_general(
                    grad, win[slot, :, cols], (((1,), (1,)), ((), ())), preferred_element_type=F32
                )
                prod = prod * keep[slot]
                both = prod if both is None else both + prod
            slabs = [both[8 * q : 8 * q + 8] for q in range(16)]
            while len(slabs) > 1:
                half = len(slabs) // 2
                slabs = [
                    slabs[q] + pltpu.roll(slabs[q + half], 2 * SPAN - 8 * half, 1)
                    for q in range(half)
                ]
            rows = pl.ds(pl.multiple_of(t * 64 + u * 8, 8), 8)
            diag[0, rows, :] = slabs[0][:, :LANES]
            diag[1, rows, :] = slabs[0][:, LANES:]
        return carry

    lax.fori_loop(0, tiles, taps, 0)
    groups = gf_ref.shape[0]
    total = None
    for r in range(8):
        row = jnp.concatenate([diag[n, pl.ds(r, groups, stride=8), :] for n in range(2)], axis=1)
        total = row if r == 0 else total + pltpu.roll(row, 2 * SPAN - r, 1)
    total = pltpu.roll(total, 2 * SPAN - 1, 1)[:, :LANES]

    copies = []
    for n, buffer in enumerate((tap_y, tap_z, tap_x)):
        buffer[0] = total
        sent = [
            pltpu.make_async_remote_copy(
                src_ref=buffer.at[0],
                dst_ref=buffer.at[i + 1],
                send_sem=tap_send.at[n, i],
                recv_sem=tap_recv.at[n, i],
                device_id=(target, tp),
                device_id_type=MESH,
            )
            for i, target in enumerate(partners[n])
        ]
        for copy in sent:
            copy.start()
        for copy in sent:
            copy.wait_recv()
        if n < 2:
            total = (buffer[0] + buffer[2]) + (buffer[1] + buffer[3])
        else:
            total = buffer[0] + buffer[1]
        copies += sent
    gf_ref[...] = total
    for copy in copies:
        copy.wait_send()


def back_call(doc_lens, filters, qkv, prev, dc, dcn, gq, count):
    groups = filters.shape[0]
    width = qkv.shape[2]
    return pl.pallas_call(
        functools.partial(back_kernel, count),
        out_shape=(
            jax.ShapeDtypeStruct(qkv.shape, BF16),
            jax.ShapeDtypeStruct((groups, LANES), F32),
        ),
        in_specs=[pl.BlockSpec(memory_space=pltpu.SMEM)]
        + [pl.BlockSpec(memory_space=pltpu.VMEM)] * 6,
        out_specs=(pl.BlockSpec(memory_space=pltpu.VMEM),) * 2,
        scratch_shapes=[
            pltpu.VMEM((2, 8 * groups, SPAN), F32),
            pltpu.VMEM((groups, SPAN, 2 * SPAN), BF16),
            pltpu.VMEM((2, SPAN, 2 * SPAN), BF16),
            pltpu.VMEM((2, SPAN, 2 * SPAN), F32),
            pltpu.VMEM((2, 2 * SPAN, width), BF16),
            pltpu.VMEM((2, 2 * SPAN, width), BF16),
            pltpu.VMEM((2, 8 * groups, SPAN), F32),
            pltpu.VMEM((4, groups, LANES), F32),
            pltpu.VMEM((4, groups, LANES), F32),
            pltpu.VMEM((2, groups, LANES), F32),
            pltpu.SemaphoreType.DMA((3, 3)),
            pltpu.SemaphoreType.DMA((3, 3)),
        ],
        compiler_params=pltpu.CompilerParams(
            vmem_limit_bytes=40 * 1024 * 1024, collective_id=1, has_side_effects=True
        ),
        name="back",
    )(doc_lens, filters, qkv, prev, dc, dcn, gq)


def project_kernel(
    scale,
    cot_ref,
    yt_ref,
    w_ref,
    qkv_ref,
    c_ref,
    gw_ref,
    dc_ref,
    gq_ref,
    full,
    w_v,
    q_v,
    part,
    relay1,
    done1,
    red,
    relay2,
    done2,
    away,
    kept,
    far,
    load_sem,
    cot_send,
    cot_recv,
    send1,
    recv1,
    send2,
    recv2,
    far_send,
    far_recv,
):
    ctx = lax.axis_index("ctx")
    tp = lax.axis_index("tp")
    my_y = ctx % 4
    my_z = (ctx // 4) % 4
    my_x = ctx // 16
    place = (my_y, my_z)
    stride = (1, 4)
    rows_local = cot_ref.shape[0]

    def around(axis, step):
        return ctx + stride[axis] * ((place[axis] + step) % 4 - place[axis])

    across = ctx + 16 - 32 * my_x
    core = tp + 1 - 2 * (tp % 2)
    beside = tp + 2 - 4 * (tp // 2)

    barrier = pltpu.get_barrier_semaphore()
    for axis in range(2):
        for step in (1, 3):
            pl.semaphore_signal(
                barrier, inc=1, device_id=(around(axis, step), tp), device_id_type=MESH
            )
    pl.semaphore_signal(barrier, inc=1, device_id=(across, tp), device_id_type=MESH)
    pl.semaphore_signal(barrier, inc=1, device_id=(ctx, core), device_id_type=MESH)
    pl.semaphore_signal(barrier, inc=1, device_id=(ctx, beside), device_id_type=MESH)
    load_w = pltpu.make_async_copy(w_ref, w_v, load_sem.at[0])
    load_q = pltpu.make_async_copy(qkv_ref.at[0], q_v, load_sem.at[1])
    pl.semaphore_wait(barrier, 7)

    half_cols = cot_ref.shape[1] // 2
    col0 = [
        pl.multiple_of((1 - my_x) * half_cols, half_cols),
        pl.multiple_of(my_x * half_cols, half_cols),
    ]

    def cot_copy(k, n, src, owner, target):
        rows = pl.ds(pl.multiple_of(owner * rows_local, rows_local), rows_local)
        cols = pl.ds(col0[k], half_cols)
        return pltpu.make_async_remote_copy(
            src_ref=cot_ref.at[:, cols] if src is None else full.at[rows, cols],
            dst_ref=full.at[rows, cols],
            send_sem=cot_send.at[k, n],
            recv_sem=cot_recv.at[k, n],
            device_id=(ctx, target),
            device_id_type=MESH,
        )

    side = [cot_copy(k, 0, None, tp, beside) for k in range(2)]
    near = [cot_copy(k, 1, None, tp, core) for k in range(2)]
    pass_on = [cot_copy(k, 2, full, beside, core) for k in range(2)]
    for k in range(2):
        side[k].start()
        near[k].start()
    load_w.start()
    load_q.start()
    full[pl.ds(pl.multiple_of(tp * rows_local, rows_local), rows_local), :] = cot_ref[...]

    def gather(k):
        side[k].wait_recv()
        pass_on[k].start()
        near[k].wait_recv()
        pass_on[k].wait_recv()

    def partial(k):
        def block(i, carry):
            tokens = full[:, pl.ds(pl.multiple_of(col0[k] + i * 256, 256), 256)]

            def some(m, inner):
                rows = pl.ds(pl.multiple_of(m * 256, 256), 256)
                out = jnp.dot(yt_ref[rows, :], tokens, preferred_element_type=F32).astype(BF16)
                part[k, i // 2, (i % 2) * 2, rows, :] = out[:, :LANES]
                part[k, i // 2, (i % 2) * 2 + 1, rows, :] = out[:, LANES:]
                return inner

            return lax.fori_loop(0, 4, some, carry)

        lax.fori_loop(0, 8, block, 0)

    def quarter(axis, half):
        first = axis * 512 + half * 256
        return slice(first, first + 256)

    def piece1(axis, k, j, half):
        if axis == 0:
            return part.at[k, :, j, quarter(axis, half)]
        return part.at[k, j, :, quarter(axis, half)]

    def piece2(axis, k, j, half):
        return red.at[axis, k, j, pl.ds(half * 256, 256)]

    def ring(stage, axis, k):
        ring_axis = axis if stage == 1 else 1 - axis
        m = place[ring_axis]
        up, down = around(ring_axis, 1), around(ring_axis, 3)
        piece = piece1 if stage == 1 else piece2
        relays = relay1 if stage == 1 else relay2
        done = done1 if stage == 1 else done2
        send, recv = (send1, recv1) if stage == 1 else (send2, recv2)
        nxt, prv, opp = (m + 1) % 4, (m + 3) % 4, (m + 2) % 4
        table = [
            (piece(axis, k, opp, 0), relays.at[axis, k, 0], up),
            (piece(axis, k, opp, 1), relays.at[axis, k, 1], down),
            (piece(axis, k, nxt, 1), done.at[axis, k, 0], up),
            (piece(axis, k, prv, 0), done.at[axis, k, 1], down),
            (piece(axis, k, nxt, 0), done.at[axis, k, 2], up),
            (piece(axis, k, prv, 1), done.at[axis, k, 3], down),
        ]
        copies = [
            pltpu.make_async_remote_copy(
                src_ref=src,
                dst_ref=dst,
                send_sem=send.at[axis, k, n],
                recv_sem=recv.at[axis, k, n],
                device_id=(target, tp),
                device_id_type=MESH,
            )
            for n, (src, dst, target) in enumerate(table)
        ]

        def start():
            for n in range(4):
                copies[n].start()

        def forward():
            for n in range(2):
                copies[n].wait_recv()
                mine = piece(axis, k, nxt if n == 0 else prv, n)
                mine[...] = (mine[...].astype(F32) + relays[axis, k, n].astype(F32)).astype(BF16)
                copies[4 + n].start()

        def finish(half):
            copies[3 if half == 0 else 2].wait_recv()
            copies[4 if half == 0 else 5].wait_recv()
            total = piece(axis, k, m, half)[...].astype(F32)
            total = total + done[axis, k, 1 if half == 0 else 0].astype(F32)
            return total + done[axis, k, 2 if half == 0 else 3].astype(F32)

        return start, forward, finish, copies

    first = [[ring(1, axis, k) for axis in range(2)] for k in range(2)]
    second = [[ring(2, axis, k) for axis in range(2)] for k in range(2)]

    for k in range(2):
        gather(k)
        partial(k)
        for axis in range(2):
            first[k][axis][0]()

    load_w.wait()
    load_q.wait()

    def project(n, carry):
        cols = pl.ds(pl.multiple_of(n * 256, 256), 256)
        dy = jnp.dot(full[...], w_v[:, cols], preferred_element_type=F32)
        dc_ref[:, cols] = (q_v[:, cols].astype(F32) * dy).astype(BF16)
        gq_ref[:, cols] = (dy * c_ref[:, cols]).astype(BF16)
        return carry

    lax.fori_loop(0, 4, project, 0)

    for k in range(2):
        for axis in range(2):
            first[k][axis][1]()
    for k in range(2):
        for axis in range(2):
            for half in range(2):
                red[axis, k, :, half * 256 : half * 256 + 256, :] = first[k][axis][2](half).astype(
                    BF16
                )
            second[k][axis][0]()
    for k in range(2):
        for axis in range(2):
            second[k][axis][1]()
    for k in range(2):
        for axis in range(2):
            for half in range(2):
                total = second[k][axis][2](half)
                if k == 0:
                    away[quarter(axis, half)] = total.astype(BF16)
                else:
                    kept[quarter(axis, half)] = total
        if k == 0:
            over = pltpu.make_async_remote_copy(
                src_ref=away,
                dst_ref=far,
                send_sem=far_send,
                recv_sem=far_recv,
                device_id=(across, tp),
                device_id_type=MESH,
            )
            over.start()
    over.wait_recv()
    for n in range(8):
        rows = slice(n * LANES, (n + 1) * LANES)
        gw_ref[:, rows] = ((kept[rows] + far[rows].astype(F32)) * scale).T
    over.wait_send()
    for k in range(2):
        side[k].wait_send()
        near[k].wait_send()
        pass_on[k].wait_send()
        for axis in range(2):
            for copy in first[k][axis][3] + second[k][axis][3]:
                copy.wait_send()


def project_call(cot, yt, w_out, qkv, c, scale):
    rows_local, feats = cot.shape
    width = w_out.shape[1]
    tokens = qkv.shape[1]
    vm = pl.BlockSpec(memory_space=pltpu.VMEM)
    hb = pl.BlockSpec(memory_space=pl.ANY)
    return pl.pallas_call(
        functools.partial(project_kernel, scale),
        out_shape=(
            jax.ShapeDtypeStruct((feats // 32, width), F32),
            jax.ShapeDtypeStruct((tokens, width), BF16),
            jax.ShapeDtypeStruct((tokens, width), BF16),
        ),
        in_specs=[vm, vm, hb, hb, vm],
        out_specs=(vm, vm, vm),
        scratch_shapes=[
            pltpu.VMEM((tokens, feats), BF16),
            pltpu.VMEM((feats, width), BF16),
            pltpu.VMEM((tokens, width), BF16),
            pltpu.VMEM((2, 4, 4, width, LANES), BF16),
            pltpu.VMEM((2, 2, 2, 4, 256, LANES), BF16),
            pltpu.VMEM((2, 2, 4, 4, 256, LANES), BF16),
            pltpu.VMEM((2, 2, 4, 512, LANES), BF16),
            pltpu.VMEM((2, 2, 2, 256, LANES), BF16),
            pltpu.VMEM((2, 2, 4, 256, LANES), BF16),
            pltpu.VMEM((width, LANES), BF16),
            pltpu.VMEM((width, LANES), F32),
            pltpu.VMEM((width, LANES), BF16),
            pltpu.SemaphoreType.DMA((2,)),
            pltpu.SemaphoreType.DMA((2, 3)),
            pltpu.SemaphoreType.DMA((2, 3)),
            pltpu.SemaphoreType.DMA((2, 2, 6)),
            pltpu.SemaphoreType.DMA((2, 2, 6)),
            pltpu.SemaphoreType.DMA((2, 2, 6)),
            pltpu.SemaphoreType.DMA((2, 2, 6)),
            pltpu.SemaphoreType.DMA,
            pltpu.SemaphoreType.DMA,
        ],
        compiler_params=pltpu.CompilerParams(
            vmem_limit_bytes=60 * 1024 * 1024, collective_id=0, has_side_effects=True
        ),
        name="project",
    )(cot, yt, w_out, qkv, c)


def neighbours(low, high, count):
    ahead = lax.ppermute(low, "ctx", [(i, i + 1) for i in range(count - 1)])
    behind = lax.ppermute(high, "ctx", [(i + 1, i) for i in range(count - 1)])
    return ahead, behind


def local(qkv, filters, w_out, cotangent, doc_lens):
    count = lax.axis_size("ctx")
    last = lax.axis_index("ctx") == count - 1
    tokens = qkv.shape[1] * count
    scale = 1.0 / math.sqrt(tokens)
    hidden = (qkv[1].astype(F32) * qkv[2].astype(F32)).astype(BF16)
    before, after = neighbours(hidden[:SPAN], hidden[SPAN:], count)
    prev = jnp.stack([before, jnp.where(last, hidden[:SPAN], after)])
    conv, gated = conv_call(doc_lens, filters, qkv, prev, count)
    grad_w, grad_c, grad_q = project_call(cotangent, gated, w_out, qkv, conv, scale)
    before, after = neighbours(grad_c[SPAN:], grad_c[:SPAN], count)
    follow = jnp.stack([jnp.where(last, grad_c[SPAN:], after), before])
    grad_qkv, taps = back_call(doc_lens, filters, qkv, prev, grad_c, follow, grad_q, count)
    return grad_qkv, jnp.flip(taps, axis=1) * scale, grad_w


def solution(mesh):
    return jax.shard_map(
        local,
        mesh=mesh,
        in_specs=(P(None, "ctx", "tp"), P("tp", None), P(None, "tp"), P(("ctx", "tp"), None), P()),
        out_specs=(P(None, "ctx", "tp"), P("tp", None), P("ctx", "tp")),
        check_vma=False,
    )
```

```python
import functools
import math

import jax
import jax.numpy as jnp
from jax import lax
from jax.experimental import pallas as pl
from jax.experimental.pallas import tpu as pltpu
from jax.sharding import PartitionSpec as P

F32 = jnp.float32
BF16 = jnp.bfloat16
MESH = pl.DeviceIdType.MESH
BIG = 64 * 1024 * 1024 - 65536
SPAN = 128
LANES = 128


def doc_starts_row(doc_ref, pos):
    def step(d, carry):
        start, best = carry
        best = jnp.where(pos >= start, start, best)
        return start + doc_ref[d], best

    return lax.fori_loop(0, doc_ref.shape[0], step, (jnp.int32(0), jnp.zeros_like(pos)))[1]


def as_column(row):
    return jnp.broadcast_to(row.astype(F32), (LANES, LANES)).T.astype(jnp.int32)


def sheared(padded, base_ref):
    groups = padded.shape[0]
    for r in range(8):
        turned = padded if r == 0 else pltpu.roll(padded, r, 1)
        for n in range(2):
            base_ref[n, pl.ds(r, groups, stride=8), :] = turned[:, n * LANES : (n + 1) * LANES]


def toeplitz(base_ref, out_ref):
    def one(g, carry):
        rows = pl.ds(pl.multiple_of(g * 8, 8), 8)
        slab = jnp.concatenate([base_ref[0, rows, :], base_ref[1, rows, :]], axis=1)
        for q in range(0, 16, 2):
            low = slab if q == 0 else pltpu.roll(slab, 8 * q, 1)
            high = pltpu.roll(slab, 8 * q + 8, 1)
            out_ref[g, 8 * q : 8 * q + 16, :] = jnp.concatenate([low, high], axis=0).astype(BF16)
        return carry

    lax.fori_loop(0, out_ref.shape[0], one, 0)


def flipped(filters):
    row = lax.broadcasted_iota(jnp.int32, (LANES, LANES), 0)
    col = lax.broadcasted_iota(jnp.int32, (LANES, LANES), 1)
    anti = (row + col == LANES - 1).astype(F32).astype(BF16)
    return jnp.dot(filters, anti, preferred_element_type=F32)


def block_position(slot, rank, count):
    return (rank if slot == 0 else 2 * count - 1 - rank) * SPAN


def window_mask(doc_ref, start):
    lane = lax.broadcasted_iota(jnp.int32, (1, LANES), 1)
    begins = as_column(doc_starts_row(doc_ref, lane + start))
    begins = jnp.concatenate([begins, begins], axis=1)
    col = lax.broadcasted_iota(jnp.int32, (SPAN, 2 * SPAN), 1) + (start - SPAN)
    return (col >= begins).astype(jnp.int32)


def spread_mask(doc_ref, start, next_start):
    lane = lax.broadcasted_iota(jnp.int32, (1, LANES), 1)
    begins = jnp.concatenate(
        [doc_starts_row(doc_ref, lane + start), doc_starts_row(doc_ref, lane + next_start)], axis=1
    )
    row = lax.broadcasted_iota(jnp.int32, (SPAN, 2 * SPAN), 0) + start
    return (row >= jnp.broadcast_to(begins, (SPAN, 2 * SPAN))).astype(jnp.int32)


def halo_copies(sources, edge, targets, send, recv):
    tp = lax.axis_index("tp")
    return [
        pltpu.make_async_remote_copy(
            src_ref=sources[slot],
            dst_ref=edge.at[slot],
            send_sem=send.at[slot],
            recv_sem=recv.at[slot],
            device_id=(targets[slot], tp),
            device_id_type=MESH,
        )
        for slot in range(2)
    ]


def conv_kernel(
    count,
    doc_ref,
    filt_ref,
    qkv_ref,
    c_ref,
    yt_ref,
    win,
    base,
    toep,
    mask,
    own,
    edge,
    edge_send,
    edge_recv,
):
    rank = lax.axis_index("ctx")
    ends = ((rank + 1) % count, (rank + count - 1) % count)
    barrier = pltpu.get_barrier_semaphore()
    for target in ends:
        pl.semaphore_signal(
            barrier, inc=1, device_id=(target, lax.axis_index("tp")), device_id_type=MESH
        )
    for slot in range(2):
        rows = slice(slot * SPAN, (slot + 1) * SPAN)
        own[slot] = (qkv_ref[1, rows].astype(F32) * qkv_ref[2, rows].astype(F32)).astype(BF16)
    pl.semaphore_wait(barrier, 2)
    halo = halo_copies([own.at[0], own.at[1]], edge, ends, edge_send, edge_recv)
    for copy in halo:
        copy.start()
    flip = flipped(filt_ref[...])
    sheared(pltpu.roll(jnp.concatenate([flip, jnp.zeros_like(flip)], axis=1), 1, 1), base)
    toeplitz(base, toep)
    for slot in range(2):
        mask[slot] = (
            window_mask(doc_ref, block_position(slot, rank, count)).astype(F32).astype(BF16)
        )
    for slot in range(2):
        halo[slot].wait_recv()
        win[slot, SPAN:] = own[slot]
    win[0, :SPAN] = edge[0]
    win[1, :SPAN] = jnp.where(rank == count - 1, own[0], edge[1])
    owner = lax.broadcasted_iota(jnp.int32, (SPAN, LANES), 1) // 16
    tiles = c_ref.shape[1] // LANES

    def tile(n, carry):
        slot, t = n // tiles, n % tiles
        cols = pl.ds(pl.multiple_of(t * LANES, LANES), LANES)
        rows = pl.ds(pl.multiple_of(slot * SPAN, SPAN), SPAN)
        window = win[slot, :, cols]
        keep = mask[slot]
        total = jnp.zeros((SPAN, LANES), F32)
        for u in range(8):
            part = jnp.dot(toep[t * 8 + u] * keep, window, preferred_element_type=F32)
            total = jnp.where(owner == u, part, total)
        c_ref[rows, cols] = total
        gated = (qkv_ref[0, rows, cols].astype(F32) * total).astype(BF16).astype(F32)
        yt_ref[cols, rows] = gated.T.astype(BF16)
        return carry

    lax.fori_loop(0, 2 * tiles, tile, 0)
    for copy in halo:
        copy.wait_send()


def conv_call(doc_lens, filters, qkv, count):
    groups = filters.shape[0]
    width = qkv.shape[2]
    return pl.pallas_call(
        functools.partial(conv_kernel, count),
        out_shape=(
            jax.ShapeDtypeStruct((2 * SPAN, width), F32),
            jax.ShapeDtypeStruct((width, 2 * SPAN), BF16),
            jax.ShapeDtypeStruct((2, 2 * SPAN, width), BF16),
        ),
        in_specs=[pl.BlockSpec(memory_space=pltpu.SMEM)]
        + [pl.BlockSpec(memory_space=pltpu.VMEM)] * 2,
        out_specs=(pl.BlockSpec(memory_space=pltpu.VMEM),) * 3,
        scratch_shapes=[
            pltpu.VMEM((2, 8 * groups, SPAN), F32),
            pltpu.VMEM((groups, SPAN, 2 * SPAN), BF16),
            pltpu.VMEM((2, SPAN, 2 * SPAN), BF16),
            pltpu.VMEM((2, SPAN, width), BF16),
            pltpu.VMEM((2, SPAN, width), BF16),
            pltpu.SemaphoreType.DMA((2,)),
            pltpu.SemaphoreType.DMA((2,)),
        ],
        compiler_params=pltpu.CompilerParams(
            vmem_limit_bytes=40 * 1024 * 1024, collective_id=2, has_side_effects=True
        ),
        name="conv",
    )(doc_lens, filters, qkv)


def back_kernel(
    count,
    doc_ref,
    filt_ref,
    qkv_ref,
    win,
    dc_ref,
    gq_ref,
    out_ref,
    gf_ref,
    base,
    toep,
    spread,
    keep,
    dwin,
    edge,
    diag,
    tap_y,
    tap_z,
    tap_x,
    tap_send,
    tap_recv,
    edge_send,
    edge_recv,
):
    rank = lax.axis_index("ctx")
    tp = lax.axis_index("tp")
    place = (rank % 4, (rank // 4) % 4)
    across = rank + 16 - 32 * (rank // 16)

    def around(axis, step):
        return rank + (1, 4)[axis] * ((place[axis] + step) % 4 - place[axis])

    partners = [[around(axis, step) for step in (1, 2, 3)] for axis in range(2)] + [[across]]
    barrier = pltpu.get_barrier_semaphore()
    for targets in partners:
        for target in targets:
            pl.semaphore_signal(barrier, inc=1, device_id=(target, tp), device_id_type=MESH)
    ends = ((rank + count - 1) % count, (rank + 1) % count)
    for target in ends:
        pl.semaphore_signal(barrier, inc=1, device_id=(target, tp), device_id_type=MESH)
    pl.semaphore_wait(barrier, 9)
    halo = halo_copies(
        [dc_ref.at[slot * SPAN : (slot + 1) * SPAN] for slot in range(2)],
        edge,
        ends,
        edge_send,
        edge_recv,
    )
    for copy in halo:
        copy.start()
    out_ref[0] = gq_ref[...]
    for slot in range(2):
        start = block_position(slot, rank, count)
        follow = (rank + 1) * SPAN if slot == 0 else (2 * count - rank) * SPAN
        keep[slot] = window_mask(doc_ref, start).astype(F32)
        spread[slot] = spread_mask(doc_ref, start, follow).astype(F32).astype(BF16)
        rows = slice(slot * SPAN, (slot + 1) * SPAN)
        dwin[slot, :SPAN] = dc_ref[rows]
    owner = lax.broadcasted_iota(jnp.int32, (SPAN, LANES), 1) // 16
    tiles = dc_ref.shape[1] // LANES

    def tile(n, carry):
        slot, t = n // tiles, n % tiles
        cols = pl.ds(pl.multiple_of(t * LANES, LANES), LANES)
        rows = pl.ds(pl.multiple_of(slot * SPAN, SPAN), SPAN)
        window = dwin[slot, :, cols]
        mask = spread[slot]
        total = jnp.zeros((SPAN, LANES), F32)
        for u in range(8):
            part = jnp.dot(toep[t * 8 + u] * mask, window, preferred_element_type=F32)
            total = jnp.where(owner == u, part, total)
        out_ref[1, rows, cols] = (total * qkv_ref[2, rows, cols].astype(F32)).astype(BF16)
        out_ref[2, rows, cols] = (total * qkv_ref[1, rows, cols].astype(F32)).astype(BF16)
        return carry

    def taps(t, carry):
        cols = pl.ds(pl.multiple_of(t * LANES, LANES), LANES)
        for u in range(8):
            both = None
            for slot in range(2):
                grad = dwin[slot, :SPAN, cols].astype(F32)
                grad = jnp.where(owner == u, grad, 0.0).astype(BF16)
                prod = lax.dot_general(
                    grad, win[slot, :, cols], (((1,), (1,)), ((), ())), preferred_element_type=F32
                )
                prod = prod * keep[slot]
                both = prod if both is None else both + prod
            slabs = [both[8 * q : 8 * q + 8] for q in range(16)]
            while len(slabs) > 1:
                half = len(slabs) // 2
                slabs = [
                    slabs[q] + pltpu.roll(slabs[q + half], 2 * SPAN - 8 * half, 1)
                    for q in range(half)
                ]
            rows = pl.ds(pl.multiple_of(t * 64 + u * 8, 8), 8)
            diag[0, rows, :] = slabs[0][:, :LANES]
            diag[1, rows, :] = slabs[0][:, LANES:]
        return carry

    lax.fori_loop(0, tiles, taps, 0)
    groups = gf_ref.shape[0]
    total = None
    for r in range(8):
        row = jnp.concatenate([diag[n, pl.ds(r, groups, stride=8), :] for n in range(2)], axis=1)
        total = row if r == 0 else total + pltpu.roll(row, 2 * SPAN - r, 1)
    total = pltpu.roll(total, 2 * SPAN - 1, 1)[:, :LANES]

    buffers = (tap_y, tap_z, tap_x)
    taken = [
        [
            pltpu.make_async_remote_copy(
                src_ref=buffers[n].at[0],
                dst_ref=buffers[n].at[i + 1],
                send_sem=tap_send.at[n, i],
                recv_sem=tap_recv.at[n, i],
                device_id=(target, tp),
                device_id_type=MESH,
            )
            for i, target in enumerate(partners[n])
        ]
        for n in range(3)
    ]

    def give(n, value):
        buffers[n][0] = value
        for copy in taken[n]:
            copy.start()

    def take(n):
        for copy in taken[n]:
            copy.wait_recv()
        if n == 2:
            return tap_x[0] + tap_x[1]
        return (buffers[n][0] + buffers[n][2]) + (buffers[n][1] + buffers[n][3])

    give(0, total)
    filt = filt_ref[...].astype(F32)
    sheared(jnp.concatenate([filt, jnp.zeros_like(filt)], axis=1), base)
    toeplitz(base, toep)
    give(1, take(0))
    for slot in range(2):
        halo[slot].wait_recv()
    dwin[0, SPAN:] = jnp.where(rank == count - 1, dc_ref[SPAN:], edge[0])
    dwin[1, SPAN:] = jnp.where(rank == 0, jnp.zeros_like(edge[1]), edge[1])
    lax.fori_loop(0, tiles, tile, 0)
    give(2, take(1))
    lax.fori_loop(tiles, 2 * tiles, tile, 0)
    gf_ref[...] = take(2)
    for copy in halo + sum(taken, []):
        copy.wait_send()


def back_call(doc_lens, filters, qkv, win, dc, gq, count):
    groups = filters.shape[0]
    width = qkv.shape[2]
    return pl.pallas_call(
        functools.partial(back_kernel, count),
        out_shape=(
            jax.ShapeDtypeStruct(qkv.shape, BF16),
            jax.ShapeDtypeStruct((groups, LANES), F32),
        ),
        in_specs=[pl.BlockSpec(memory_space=pltpu.SMEM)]
        + [pl.BlockSpec(memory_space=pltpu.VMEM)] * 5,
        out_specs=(pl.BlockSpec(memory_space=pltpu.VMEM),) * 2,
        scratch_shapes=[
            pltpu.VMEM((2, 8 * groups, SPAN), F32),
            pltpu.VMEM((groups, SPAN, 2 * SPAN), BF16),
            pltpu.VMEM((2, SPAN, 2 * SPAN), BF16),
            pltpu.VMEM((2, SPAN, 2 * SPAN), F32),
            pltpu.VMEM((2, 2 * SPAN, width), BF16),
            pltpu.VMEM((2, SPAN, width), BF16),
            pltpu.VMEM((2, 8 * groups, SPAN), F32),
            pltpu.VMEM((4, groups, LANES), F32),
            pltpu.VMEM((4, groups, LANES), F32),
            pltpu.VMEM((2, groups, LANES), F32),
            pltpu.SemaphoreType.DMA((3, 3)),
            pltpu.SemaphoreType.DMA((3, 3)),
            pltpu.SemaphoreType.DMA((2,)),
            pltpu.SemaphoreType.DMA((2,)),
        ],
        compiler_params=pltpu.CompilerParams(
            vmem_limit_bytes=40 * 1024 * 1024, collective_id=1, has_side_effects=True
        ),
        name="back",
    )(doc_lens, filters, qkv, win, dc, gq)


def project_kernel(
    scale,
    cot_ref,
    yt_ref,
    w_ref,
    qkv_ref,
    c_ref,
    gw_ref,
    dc_ref,
    gq_ref,
    full,
    w_v,
    q_v,
    part,
    relay1,
    done1,
    red,
    relay2,
    done2,
    away,
    kept,
    far,
    load_sem,
    cot_send,
    cot_recv,
    send1,
    recv1,
    send2,
    recv2,
    far_send,
    far_recv,
):
    ctx = lax.axis_index("ctx")
    tp = lax.axis_index("tp")
    my_y = ctx % 4
    my_z = (ctx // 4) % 4
    my_x = ctx // 16
    place = (my_y, my_z)
    stride = (1, 4)
    rows_local = cot_ref.shape[0]

    def around(axis, step):
        return ctx + stride[axis] * ((place[axis] + step) % 4 - place[axis])

    across = ctx + 16 - 32 * my_x
    core = tp + 1 - 2 * (tp % 2)
    beside = tp + 2 - 4 * (tp // 2)

    barrier = pltpu.get_barrier_semaphore()
    for axis in range(2):
        for step in (1, 3):
            pl.semaphore_signal(
                barrier, inc=1, device_id=(around(axis, step), tp), device_id_type=MESH
            )
    pl.semaphore_signal(barrier, inc=1, device_id=(across, tp), device_id_type=MESH)
    pl.semaphore_signal(barrier, inc=1, device_id=(ctx, core), device_id_type=MESH)
    pl.semaphore_signal(barrier, inc=1, device_id=(ctx, beside), device_id_type=MESH)
    load_w = pltpu.make_async_copy(w_ref, w_v, load_sem.at[0])
    load_q = pltpu.make_async_copy(qkv_ref.at[0], q_v, load_sem.at[1])
    pl.semaphore_wait(barrier, 7)

    half_cols = cot_ref.shape[1] // 2
    col0 = [
        pl.multiple_of((1 - my_x) * half_cols, half_cols),
        pl.multiple_of(my_x * half_cols, half_cols),
    ]

    def cot_copy(k, n, src, owner, target):
        rows = pl.ds(pl.multiple_of(owner * rows_local, rows_local), rows_local)
        cols = pl.ds(col0[k], half_cols)
        return pltpu.make_async_remote_copy(
            src_ref=cot_ref.at[:, cols] if src is None else full.at[rows, cols],
            dst_ref=full.at[rows, cols],
            send_sem=cot_send.at[k, n],
            recv_sem=cot_recv.at[k, n],
            device_id=(ctx, target),
            device_id_type=MESH,
        )

    side = [cot_copy(k, 0, None, tp, beside) for k in range(2)]
    near = [cot_copy(k, 1, None, tp, core) for k in range(2)]
    pass_on = [cot_copy(k, 2, full, beside, core) for k in range(2)]
    for k in range(2):
        side[k].start()
        near[k].start()
    load_w.start()
    load_q.start()
    full[pl.ds(pl.multiple_of(tp * rows_local, rows_local), rows_local), :] = cot_ref[...]

    def gather(k):
        side[k].wait_recv()
        pass_on[k].start()
        near[k].wait_recv()
        pass_on[k].wait_recv()

    def partial(k):
        def block(i, carry):
            tokens = full[:, pl.ds(pl.multiple_of(col0[k] + i * 256, 256), 256)]

            def some(m, inner):
                rows = pl.ds(pl.multiple_of(m * 256, 256), 256)
                out = jnp.dot(yt_ref[rows, :], tokens, preferred_element_type=F32).astype(BF16)
                part[k, i // 2, (i % 2) * 2, rows, :] = out[:, :LANES]
                part[k, i // 2, (i % 2) * 2 + 1, rows, :] = out[:, LANES:]
                return inner

            return lax.fori_loop(0, 4, some, carry)

        lax.fori_loop(0, 8, block, 0)

    def quarter(axis, half):
        first = axis * 512 + half * 256
        return slice(first, first + 256)

    def piece1(axis, k, j, half):
        if axis == 0:
            return part.at[k, :, j, quarter(axis, half)]
        return part.at[k, j, :, quarter(axis, half)]

    def piece2(axis, k, j, half):
        return red.at[axis, k, j, pl.ds(half * 256, 256)]

    def ring(stage, axis, k):
        ring_axis = axis if stage == 1 else 1 - axis
        m = place[ring_axis]
        up, down = around(ring_axis, 1), around(ring_axis, 3)
        piece = piece1 if stage == 1 else piece2
        relays = relay1 if stage == 1 else relay2
        done = done1 if stage == 1 else done2
        send, recv = (send1, recv1) if stage == 1 else (send2, recv2)
        nxt, prv, opp = (m + 1) % 4, (m + 3) % 4, (m + 2) % 4
        table = [
            (piece(axis, k, opp, 0), relays.at[axis, k, 0], up),
            (piece(axis, k, opp, 1), relays.at[axis, k, 1], down),
            (piece(axis, k, nxt, 1), done.at[axis, k, 0], up),
            (piece(axis, k, prv, 0), done.at[axis, k, 1], down),
            (piece(axis, k, nxt, 0), done.at[axis, k, 2], up),
            (piece(axis, k, prv, 1), done.at[axis, k, 3], down),
        ]
        copies = [
            pltpu.make_async_remote_copy(
                src_ref=src,
                dst_ref=dst,
                send_sem=send.at[axis, k, n],
                recv_sem=recv.at[axis, k, n],
                device_id=(target, tp),
                device_id_type=MESH,
            )
            for n, (src, dst, target) in enumerate(table)
        ]

        def start():
            for n in range(4):
                copies[n].start()

        def forward():
            for n in range(2):
                copies[n].wait_recv()
                mine = piece(axis, k, nxt if n == 0 else prv, n)
                mine[...] = (mine[...].astype(F32) + relays[axis, k, n].astype(F32)).astype(BF16)
                copies[4 + n].start()

        def finish(half):
            copies[3 if half == 0 else 2].wait_recv()
            copies[4 if half == 0 else 5].wait_recv()
            total = piece(axis, k, m, half)[...].astype(F32)
            total = total + done[axis, k, 1 if half == 0 else 0].astype(F32)
            return total + done[axis, k, 2 if half == 0 else 3].astype(F32)

        return start, forward, finish, copies

    first = [[ring(1, axis, k) for axis in range(2)] for k in range(2)]
    second = [[ring(2, axis, k) for axis in range(2)] for k in range(2)]

    for k in range(2):
        gather(k)
        partial(k)
        for axis in range(2):
            first[k][axis][0]()

    load_w.wait()
    load_q.wait()

    def project(n, carry):
        cols = pl.ds(pl.multiple_of(n * 256, 256), 256)
        dy = jnp.dot(full[...], w_v[:, cols], preferred_element_type=F32)
        dc_ref[:, cols] = (q_v[:, cols].astype(F32) * dy).astype(BF16)
        gq_ref[:, cols] = (dy * c_ref[:, cols]).astype(BF16)
        return carry

    lax.fori_loop(0, 4, project, 0)

    for k in range(2):
        for axis in range(2):
            first[k][axis][1]()
    for k in range(2):
        for axis in range(2):
            for half in range(2):
                red[axis, k, :, half * 256 : half * 256 + 256, :] = first[k][axis][2](half).astype(
                    BF16
                )
            second[k][axis][0]()
    for k in range(2):
        for axis in range(2):
            second[k][axis][1]()
    for k in range(2):
        for axis in range(2):
            for half in range(2):
                total = second[k][axis][2](half)
                if k == 0:
                    away[quarter(axis, half)] = total.astype(BF16)
                else:
                    kept[quarter(axis, half)] = total
        if k == 0:
            over = pltpu.make_async_remote_copy(
                src_ref=away,
                dst_ref=far,
                send_sem=far_send,
                recv_sem=far_recv,
                device_id=(across, tp),
                device_id_type=MESH,
            )
            over.start()
    over.wait_recv()
    for n in range(8):
        rows = slice(n * LANES, (n + 1) * LANES)
        gw_ref[:, rows] = ((kept[rows] + far[rows].astype(F32)) * scale).T
    over.wait_send()
    for k in range(2):
        side[k].wait_send()
        near[k].wait_send()
        pass_on[k].wait_send()
        for axis in range(2):
            for copy in first[k][axis][3] + second[k][axis][3]:
                copy.wait_send()


def project_call(cot, yt, w_out, qkv, c, scale):
    rows_local, feats = cot.shape
    width = w_out.shape[1]
    tokens = qkv.shape[1]
    vm = pl.BlockSpec(memory_space=pltpu.VMEM)
    hb = pl.BlockSpec(memory_space=pl.ANY)
    return pl.pallas_call(
        functools.partial(project_kernel, scale),
        out_shape=(
            jax.ShapeDtypeStruct((feats // 32, width), F32),
            jax.ShapeDtypeStruct((tokens, width), BF16),
            jax.ShapeDtypeStruct((tokens, width), BF16),
        ),
        in_specs=[vm, vm, hb, hb, vm],
        out_specs=(vm, vm, vm),
        scratch_shapes=[
            pltpu.VMEM((tokens, feats), BF16),
            pltpu.VMEM((feats, width), BF16),
            pltpu.VMEM((tokens, width), BF16),
            pltpu.VMEM((2, 4, 4, width, LANES), BF16),
            pltpu.VMEM((2, 2, 2, 4, 256, LANES), BF16),
            pltpu.VMEM((2, 2, 4, 4, 256, LANES), BF16),
            pltpu.VMEM((2, 2, 4, 512, LANES), BF16),
            pltpu.VMEM((2, 2, 2, 256, LANES), BF16),
            pltpu.VMEM((2, 2, 4, 256, LANES), BF16),
            pltpu.VMEM((width, LANES), BF16),
            pltpu.VMEM((width, LANES), F32),
            pltpu.VMEM((width, LANES), BF16),
            pltpu.SemaphoreType.DMA((2,)),
            pltpu.SemaphoreType.DMA((2, 3)),
            pltpu.SemaphoreType.DMA((2, 3)),
            pltpu.SemaphoreType.DMA((2, 2, 6)),
            pltpu.SemaphoreType.DMA((2, 2, 6)),
            pltpu.SemaphoreType.DMA((2, 2, 6)),
            pltpu.SemaphoreType.DMA((2, 2, 6)),
            pltpu.SemaphoreType.DMA,
            pltpu.SemaphoreType.DMA,
        ],
        compiler_params=pltpu.CompilerParams(
            vmem_limit_bytes=60 * 1024 * 1024, collective_id=0, has_side_effects=True
        ),
        name="project",
    )(cot, yt, w_out, qkv, c)


def local(qkv, filters, w_out, cotangent, doc_lens):
    count = lax.axis_size("ctx")
    tokens = qkv.shape[1] * count
    scale = 1.0 / math.sqrt(tokens)
    conv, gated, win = conv_call(doc_lens, filters, qkv, count)
    grad_w, grad_c, grad_q = project_call(cotangent, gated, w_out, qkv, conv, scale)
    grad_qkv, taps = back_call(doc_lens, filters, qkv, win, grad_c, grad_q, count)
    return grad_qkv, jnp.flip(taps, axis=1) * scale, grad_w


def solution(mesh):
    return jax.shard_map(
        local,
        mesh=mesh,
        in_specs=(P(None, "ctx", "tp"), P("tp", None), P(None, "tp"), P(("ctx", "tp"), None), P()),
        out_specs=(P(None, "ctx", "tp"), P("tp", None), P("ctx", "tp")),
        check_vma=False,
    )
```

```python
import functools
import math

import jax
import jax.numpy as jnp
from jax import lax
from jax.experimental import pallas as pl
from jax.experimental.pallas import tpu as pltpu
from jax.sharding import PartitionSpec as P

F32 = jnp.float32
BF16 = jnp.bfloat16
MESH = pl.DeviceIdType.MESH
BIG = 64 * 1024 * 1024 - 65536
SPAN = 128
LANES = 128


def doc_starts_row(doc_ref, pos):
    def step(d, carry):
        start, best = carry
        best = jnp.where(pos >= start, start, best)
        return start + doc_ref[d], best

    return lax.fori_loop(0, doc_ref.shape[0], step, (jnp.int32(0), jnp.zeros_like(pos)))[1]


def as_column(row):
    return jnp.broadcast_to(row.astype(F32), (LANES, LANES)).T.astype(jnp.int32)


def sheared(padded, base_ref):
    groups = padded.shape[0]
    for r in range(8):
        turned = padded if r == 0 else pltpu.roll(padded, r, 1)
        for n in range(2):
            base_ref[n, pl.ds(r, groups, stride=8), :] = turned[:, n * LANES : (n + 1) * LANES]


def toeplitz(base_ref, out_ref):
    def one(g, carry):
        rows = pl.ds(pl.multiple_of(g * 8, 8), 8)
        slab = jnp.concatenate([base_ref[0, rows, :], base_ref[1, rows, :]], axis=1)
        for q in range(0, 16, 2):
            low = slab if q == 0 else pltpu.roll(slab, 8 * q, 1)
            high = pltpu.roll(slab, 8 * q + 8, 1)
            out_ref[g, 8 * q : 8 * q + 16, :] = jnp.concatenate([low, high], axis=0).astype(BF16)
        return carry

    lax.fori_loop(0, out_ref.shape[0], one, 0)


def flipped(filters):
    row = lax.broadcasted_iota(jnp.int32, (LANES, LANES), 0)
    col = lax.broadcasted_iota(jnp.int32, (LANES, LANES), 1)
    anti = (row + col == LANES - 1).astype(F32).astype(BF16)
    return jnp.dot(filters, anti, preferred_element_type=F32)


def block_position(slot, rank, count):
    return (rank if slot == 0 else 2 * count - 1 - rank) * SPAN


def window_mask(doc_ref, start):
    lane = lax.broadcasted_iota(jnp.int32, (1, LANES), 1)
    begins = as_column(doc_starts_row(doc_ref, lane + start))
    begins = jnp.concatenate([begins, begins], axis=1)
    col = lax.broadcasted_iota(jnp.int32, (SPAN, 2 * SPAN), 1) + (start - SPAN)
    return (col >= begins).astype(jnp.int32)


def spread_mask(doc_ref, start, next_start):
    lane = lax.broadcasted_iota(jnp.int32, (1, LANES), 1)
    begins = jnp.concatenate(
        [doc_starts_row(doc_ref, lane + start), doc_starts_row(doc_ref, lane + next_start)], axis=1
    )
    row = lax.broadcasted_iota(jnp.int32, (SPAN, 2 * SPAN), 0) + start
    return (row >= jnp.broadcast_to(begins, (SPAN, 2 * SPAN))).astype(jnp.int32)


def halo_copies(sources, edge, targets, send, recv):
    tp = lax.axis_index("tp")
    return [
        pltpu.make_async_remote_copy(
            src_ref=sources[slot],
            dst_ref=edge.at[slot],
            send_sem=send.at[slot],
            recv_sem=recv.at[slot],
            device_id=(targets[slot], tp),
            device_id_type=MESH,
        )
        for slot in range(2)
    ]


def conv_kernel(
    count,
    doc_ref,
    filt_ref,
    qkv_ref,
    cot_ref,
    c_ref,
    yt_ref,
    win,
    full_ref,
    base,
    toep,
    mask,
    own,
    edge,
    full,
    edge_send,
    edge_recv,
    cot_send,
    cot_recv,
):
    rank = lax.axis_index("ctx")
    tp = lax.axis_index("tp")
    core = tp + 1 - 2 * (tp % 2)
    beside = tp + 2 - 4 * (tp // 2)
    rows_local = cot_ref.shape[0]
    ends = ((rank + 1) % count, (rank + count - 1) % count)
    barrier = pltpu.get_barrier_semaphore()
    for target in ends:
        pl.semaphore_signal(
            barrier, inc=1, device_id=(target, tp), device_id_type=MESH
        )
    for target in (core, beside):
        pl.semaphore_signal(barrier, inc=1, device_id=(rank, target), device_id_type=MESH)
    for slot in range(2):
        rows = slice(slot * SPAN, (slot + 1) * SPAN)
        own[slot] = (qkv_ref[1, rows].astype(F32) * qkv_ref[2, rows].astype(F32)).astype(BF16)
    pl.semaphore_wait(barrier, 4)

    def cot_copy(n, own_rows, source, target):
        rows = pl.ds(pl.multiple_of(source * rows_local, rows_local), rows_local)
        return pltpu.make_async_remote_copy(
            src_ref=cot_ref if own_rows else full.at[rows],
            dst_ref=full.at[rows],
            send_sem=cot_send.at[n],
            recv_sem=cot_recv.at[n],
            device_id=(rank, target),
            device_id_type=MESH,
        )

    side = cot_copy(0, True, tp, beside)
    near = cot_copy(1, True, tp, core)
    pass_on = cot_copy(2, False, beside, core)
    side.start()
    near.start()
    full[pl.ds(pl.multiple_of(tp * rows_local, rows_local), rows_local), :] = cot_ref[...]
    halo = halo_copies([own.at[0], own.at[1]], edge, ends, edge_send, edge_recv)
    for copy in halo:
        copy.start()
    flip = flipped(filt_ref[...])
    sheared(pltpu.roll(jnp.concatenate([flip, jnp.zeros_like(flip)], axis=1), 1, 1), base)
    toeplitz(base, toep)
    for slot in range(2):
        mask[slot] = (
            window_mask(doc_ref, block_position(slot, rank, count)).astype(F32).astype(BF16)
        )
    for slot in range(2):
        halo[slot].wait_recv()
        win[slot, SPAN:] = own[slot]
    win[0, :SPAN] = edge[0]
    win[1, :SPAN] = jnp.where(rank == count - 1, own[0], edge[1])
    owner = lax.broadcasted_iota(jnp.int32, (SPAN, LANES), 1) // 16
    tiles = c_ref.shape[1] // LANES

    def tile(n, carry):
        slot, t = n // tiles, n % tiles
        cols = pl.ds(pl.multiple_of(t * LANES, LANES), LANES)
        rows = pl.ds(pl.multiple_of(slot * SPAN, SPAN), SPAN)
        window = win[slot, :, cols]
        keep = mask[slot]
        total = jnp.zeros((SPAN, LANES), F32)
        for u in range(8):
            part = jnp.dot(toep[t * 8 + u] * keep, window, preferred_element_type=F32)
            total = jnp.where(owner == u, part, total)
        c_ref[rows, cols] = total
        gated = (qkv_ref[0, rows, cols].astype(F32) * total).astype(BF16).astype(F32)
        yt_ref[cols, rows] = gated.T.astype(BF16)
        return carry

    lax.fori_loop(0, tiles, tile, 0)
    side.wait_recv()
    pass_on.start()
    lax.fori_loop(tiles, 2 * tiles, tile, 0)
    near.wait_recv()
    pass_on.wait_recv()
    full_ref[...] = full[...]
    for copy in halo + [side, near, pass_on]:
        copy.wait_send()


def conv_call(doc_lens, filters, qkv, cot, count):
    groups = filters.shape[0]
    width = qkv.shape[2]
    return pl.pallas_call(
        functools.partial(conv_kernel, count),
        out_shape=(
            jax.ShapeDtypeStruct((2 * SPAN, width), F32),
            jax.ShapeDtypeStruct((width, 2 * SPAN), BF16),
            jax.ShapeDtypeStruct((2, 2 * SPAN, width), BF16),
            jax.ShapeDtypeStruct((2 * SPAN, cot.shape[1]), BF16),
        ),
        in_specs=[pl.BlockSpec(memory_space=pltpu.SMEM)]
        + [pl.BlockSpec(memory_space=pltpu.VMEM)] * 3,
        out_specs=(pl.BlockSpec(memory_space=pltpu.VMEM),) * 4,
        scratch_shapes=[
            pltpu.VMEM((2, 8 * groups, SPAN), F32),
            pltpu.VMEM((groups, SPAN, 2 * SPAN), BF16),
            pltpu.VMEM((2, SPAN, 2 * SPAN), BF16),
            pltpu.VMEM((2, SPAN, width), BF16),
            pltpu.VMEM((2, SPAN, width), BF16),
            pltpu.VMEM((2 * SPAN, cot.shape[1]), BF16),
            pltpu.SemaphoreType.DMA((2,)),
            pltpu.SemaphoreType.DMA((2,)),
            pltpu.SemaphoreType.DMA((3,)),
            pltpu.SemaphoreType.DMA((3,)),
        ],
        compiler_params=pltpu.CompilerParams(
            vmem_limit_bytes=40 * 1024 * 1024, collective_id=2, has_side_effects=True
        ),
        name="conv",
    )(doc_lens, filters, qkv, cot)


def back_kernel(
    count,
    doc_ref,
    filt_ref,
    qkv_ref,
    win,
    dc_ref,
    gq_ref,
    out_ref,
    gf_ref,
    base,
    toep,
    spread,
    keep,
    dwin,
    edge,
    diag,
    tap_y,
    tap_z,
    tap_x,
    tap_send,
    tap_recv,
    edge_send,
    edge_recv,
):
    rank = lax.axis_index("ctx")
    tp = lax.axis_index("tp")
    place = (rank % 4, (rank // 4) % 4)
    across = rank + 16 - 32 * (rank // 16)

    def around(axis, step):
        return rank + (1, 4)[axis] * ((place[axis] + step) % 4 - place[axis])

    partners = [[around(axis, step) for step in (1, 2, 3)] for axis in range(2)] + [[across]]
    barrier = pltpu.get_barrier_semaphore()
    for targets in partners:
        for target in targets:
            pl.semaphore_signal(barrier, inc=1, device_id=(target, tp), device_id_type=MESH)
    ends = ((rank + count - 1) % count, (rank + 1) % count)
    for target in ends:
        pl.semaphore_signal(barrier, inc=1, device_id=(target, tp), device_id_type=MESH)
    pl.semaphore_wait(barrier, 9)
    halo = halo_copies(
        [dc_ref.at[slot * SPAN : (slot + 1) * SPAN] for slot in range(2)],
        edge,
        ends,
        edge_send,
        edge_recv,
    )
    for copy in halo:
        copy.start()
    out_ref[0] = gq_ref[...]
    for slot in range(2):
        start = block_position(slot, rank, count)
        follow = (rank + 1) * SPAN if slot == 0 else (2 * count - rank) * SPAN
        keep[slot] = window_mask(doc_ref, start).astype(F32)
        spread[slot] = spread_mask(doc_ref, start, follow).astype(F32).astype(BF16)
        rows = slice(slot * SPAN, (slot + 1) * SPAN)
        dwin[slot, :SPAN] = dc_ref[rows]
    owner = lax.broadcasted_iota(jnp.int32, (SPAN, LANES), 1) // 16
    tiles = dc_ref.shape[1] // LANES

    def tile(n, carry):
        slot, t = n // tiles, n % tiles
        cols = pl.ds(pl.multiple_of(t * LANES, LANES), LANES)
        rows = pl.ds(pl.multiple_of(slot * SPAN, SPAN), SPAN)
        window = dwin[slot, :, cols]
        mask = spread[slot]
        total = jnp.zeros((SPAN, LANES), F32)
        for u in range(8):
            part = jnp.dot(toep[t * 8 + u] * mask, window, preferred_element_type=F32)
            total = jnp.where(owner == u, part, total)
        out_ref[1, rows, cols] = (total * qkv_ref[2, rows, cols].astype(F32)).astype(BF16)
        out_ref[2, rows, cols] = (total * qkv_ref[1, rows, cols].astype(F32)).astype(BF16)
        return carry

    def taps(t, carry):
        cols = pl.ds(pl.multiple_of(t * LANES, LANES), LANES)
        for u in range(8):
            both = None
            for slot in range(2):
                grad = dwin[slot, :SPAN, cols].astype(F32)
                grad = jnp.where(owner == u, grad, 0.0).astype(BF16)
                prod = lax.dot_general(
                    grad, win[slot, :, cols], (((1,), (1,)), ((), ())), preferred_element_type=F32
                )
                prod = prod * keep[slot]
                both = prod if both is None else both + prod
            slabs = [both[8 * q : 8 * q + 8] for q in range(16)]
            while len(slabs) > 1:
                half = len(slabs) // 2
                slabs = [
                    slabs[q] + pltpu.roll(slabs[q + half], 2 * SPAN - 8 * half, 1)
                    for q in range(half)
                ]
            rows = pl.ds(pl.multiple_of(t * 64 + u * 8, 8), 8)
            diag[0, rows, :] = slabs[0][:, :LANES]
            diag[1, rows, :] = slabs[0][:, LANES:]
        return carry

    lax.fori_loop(0, tiles, taps, 0)
    groups = gf_ref.shape[0]
    total = None
    for r in range(8):
        row = jnp.concatenate([diag[n, pl.ds(r, groups, stride=8), :] for n in range(2)], axis=1)
        total = row if r == 0 else total + pltpu.roll(row, 2 * SPAN - r, 1)
    total = pltpu.roll(total, 2 * SPAN - 1, 1)[:, :LANES]

    buffers = (tap_y, tap_z, tap_x)
    taken = [
        [
            pltpu.make_async_remote_copy(
                src_ref=buffers[n].at[0],
                dst_ref=buffers[n].at[i + 1],
                send_sem=tap_send.at[n, i],
                recv_sem=tap_recv.at[n, i],
                device_id=(target, tp),
                device_id_type=MESH,
            )
            for i, target in enumerate(partners[n])
        ]
        for n in range(3)
    ]

    def give(n, value):
        buffers[n][0] = value
        for copy in taken[n]:
            copy.start()

    def take(n):
        for copy in taken[n]:
            copy.wait_recv()
        if n == 2:
            return tap_x[0] + tap_x[1]
        return (buffers[n][0] + buffers[n][2]) + (buffers[n][1] + buffers[n][3])

    give(0, total)
    filt = filt_ref[...].astype(F32)
    sheared(jnp.concatenate([filt, jnp.zeros_like(filt)], axis=1), base)
    toeplitz(base, toep)
    give(1, take(0))
    for slot in range(2):
        halo[slot].wait_recv()
    dwin[0, SPAN:] = jnp.where(rank == count - 1, dc_ref[SPAN:], edge[0])
    dwin[1, SPAN:] = jnp.where(rank == 0, jnp.zeros_like(edge[1]), edge[1])
    lax.fori_loop(0, tiles, tile, 0)
    give(2, take(1))
    lax.fori_loop(tiles, 2 * tiles, tile, 0)
    gf_ref[...] = take(2)
    for copy in halo + sum(taken, []):
        copy.wait_send()


def back_call(doc_lens, filters, qkv, win, dc, gq, count):
    groups = filters.shape[0]
    width = qkv.shape[2]
    return pl.pallas_call(
        functools.partial(back_kernel, count),
        out_shape=(
            jax.ShapeDtypeStruct(qkv.shape, BF16),
            jax.ShapeDtypeStruct((groups, LANES), F32),
        ),
        in_specs=[pl.BlockSpec(memory_space=pltpu.SMEM)]
        + [pl.BlockSpec(memory_space=pltpu.VMEM)] * 5,
        out_specs=(pl.BlockSpec(memory_space=pltpu.VMEM),) * 2,
        scratch_shapes=[
            pltpu.VMEM((2, 8 * groups, SPAN), F32),
            pltpu.VMEM((groups, SPAN, 2 * SPAN), BF16),
            pltpu.VMEM((2, SPAN, 2 * SPAN), BF16),
            pltpu.VMEM((2, SPAN, 2 * SPAN), F32),
            pltpu.VMEM((2, 2 * SPAN, width), BF16),
            pltpu.VMEM((2, SPAN, width), BF16),
            pltpu.VMEM((2, 8 * groups, SPAN), F32),
            pltpu.VMEM((4, groups, LANES), F32),
            pltpu.VMEM((4, groups, LANES), F32),
            pltpu.VMEM((2, groups, LANES), F32),
            pltpu.SemaphoreType.DMA((3, 3)),
            pltpu.SemaphoreType.DMA((3, 3)),
            pltpu.SemaphoreType.DMA((2,)),
            pltpu.SemaphoreType.DMA((2,)),
        ],
        compiler_params=pltpu.CompilerParams(
            vmem_limit_bytes=40 * 1024 * 1024, collective_id=1, has_side_effects=True
        ),
        name="back",
    )(doc_lens, filters, qkv, win, dc, gq)


def project_kernel(
    scale,
    full,
    yt_ref,
    w_ref,
    qkv_ref,
    c_ref,
    gw_ref,
    dc_ref,
    gq_ref,
    w_v,
    q_v,
    part,
    relay1,
    done1,
    red,
    relay2,
    done2,
    away,
    kept,
    far,
    load_sem,
    send1,
    recv1,
    send2,
    recv2,
    far_send,
    far_recv,
):
    ctx = lax.axis_index("ctx")
    tp = lax.axis_index("tp")
    my_y = ctx % 4
    my_z = (ctx // 4) % 4
    my_x = ctx // 16
    place = (my_y, my_z)
    stride = (1, 4)

    def around(axis, step):
        return ctx + stride[axis] * ((place[axis] + step) % 4 - place[axis])

    across = ctx + 16 - 32 * my_x

    barrier = pltpu.get_barrier_semaphore()
    for axis in range(2):
        for step in (1, 3):
            pl.semaphore_signal(
                barrier, inc=1, device_id=(around(axis, step), tp), device_id_type=MESH
            )
    pl.semaphore_signal(barrier, inc=1, device_id=(across, tp), device_id_type=MESH)
    load_w = pltpu.make_async_copy(w_ref, w_v, load_sem.at[0])
    load_q = pltpu.make_async_copy(qkv_ref.at[0], q_v, load_sem.at[1])
    pl.semaphore_wait(barrier, 5)

    half_cols = full.shape[1] // 2
    col0 = [
        pl.multiple_of((1 - my_x) * half_cols, half_cols),
        pl.multiple_of(my_x * half_cols, half_cols),
    ]

    load_w.start()
    load_q.start()

    def partial(k):
        def block(i, carry):
            tokens = full[:, pl.ds(pl.multiple_of(col0[k] + i * 256, 256), 256)]

            def some(m, inner):
                rows = pl.ds(pl.multiple_of(m * 256, 256), 256)
                out = jnp.dot(yt_ref[rows, :], tokens, preferred_element_type=F32).astype(BF16)
                part[k, i // 2, (i % 2) * 2, rows, :] = out[:, :LANES]
                part[k, i // 2, (i % 2) * 2 + 1, rows, :] = out[:, LANES:]
                return inner

            return lax.fori_loop(0, 4, some, carry)

        lax.fori_loop(0, 8, block, 0)

    def quarter(axis, half):
        first = axis * 512 + half * 256
        return slice(first, first + 256)

    def piece1(axis, k, j, half):
        if axis == 0:
            return part.at[k, :, j, quarter(axis, half)]
        return part.at[k, j, :, quarter(axis, half)]

    def piece2(axis, k, j, half):
        return red.at[axis, k, j, pl.ds(half * 256, 256)]

    def ring(stage, axis, k):
        ring_axis = axis if stage == 1 else 1 - axis
        m = place[ring_axis]
        up, down = around(ring_axis, 1), around(ring_axis, 3)
        piece = piece1 if stage == 1 else piece2
        relays = relay1 if stage == 1 else relay2
        done = done1 if stage == 1 else done2
        send, recv = (send1, recv1) if stage == 1 else (send2, recv2)
        nxt, prv, opp = (m + 1) % 4, (m + 3) % 4, (m + 2) % 4
        table = [
            (piece(axis, k, opp, 0), relays.at[axis, k, 0], up),
            (piece(axis, k, opp, 1), relays.at[axis, k, 1], down),
            (piece(axis, k, nxt, 1), done.at[axis, k, 0], up),
            (piece(axis, k, prv, 0), done.at[axis, k, 1], down),
            (piece(axis, k, nxt, 0), done.at[axis, k, 2], up),
            (piece(axis, k, prv, 1), done.at[axis, k, 3], down),
        ]
        copies = [
            pltpu.make_async_remote_copy(
                src_ref=src,
                dst_ref=dst,
                send_sem=send.at[axis, k, n],
                recv_sem=recv.at[axis, k, n],
                device_id=(target, tp),
                device_id_type=MESH,
            )
            for n, (src, dst, target) in enumerate(table)
        ]

        def start():
            for n in range(4):
                copies[n].start()

        def forward():
            for n in range(2):
                copies[n].wait_recv()
                mine = piece(axis, k, nxt if n == 0 else prv, n)
                mine[...] = (mine[...].astype(F32) + relays[axis, k, n].astype(F32)).astype(BF16)
                copies[4 + n].start()

        def finish(half):
            copies[3 if half == 0 else 2].wait_recv()
            copies[4 if half == 0 else 5].wait_recv()
            total = piece(axis, k, m, half)[...].astype(F32)
            total = total + done[axis, k, 1 if half == 0 else 0].astype(F32)
            return total + done[axis, k, 2 if half == 0 else 3].astype(F32)

        return start, forward, finish, copies

    first = [[ring(1, axis, k) for axis in range(2)] for k in range(2)]
    second = [[ring(2, axis, k) for axis in range(2)] for k in range(2)]

    for k in range(2):
        partial(k)
        for axis in range(2):
            first[k][axis][0]()

    load_w.wait()
    load_q.wait()

    def project(n, carry):
        cols = pl.ds(pl.multiple_of(n * 256, 256), 256)
        dy = jnp.dot(full[...], w_v[:, cols], preferred_element_type=F32)
        dc_ref[:, cols] = (q_v[:, cols].astype(F32) * dy).astype(BF16)
        gq_ref[:, cols] = (dy * c_ref[:, cols]).astype(BF16)
        return carry

    lax.fori_loop(0, 4, project, 0)

    for k in range(2):
        for axis in range(2):
            first[k][axis][1]()
    for k in range(2):
        for axis in range(2):
            for half in range(2):
                red[axis, k, :, half * 256 : half * 256 + 256, :] = first[k][axis][2](half).astype(
                    BF16
                )
            second[k][axis][0]()
    for k in range(2):
        for axis in range(2):
            second[k][axis][1]()
    for k in range(2):
        for axis in range(2):
            for half in range(2):
                total = second[k][axis][2](half)
                if k == 0:
                    away[quarter(axis, half)] = total.astype(BF16)
                else:
                    kept[quarter(axis, half)] = total
        if k == 0:
            over = pltpu.make_async_remote_copy(
                src_ref=away,
                dst_ref=far,
                send_sem=far_send,
                recv_sem=far_recv,
                device_id=(across, tp),
                device_id_type=MESH,
            )
            over.start()
    over.wait_recv()
    for n in range(8):
        rows = slice(n * LANES, (n + 1) * LANES)
        gw_ref[:, rows] = ((kept[rows] + far[rows].astype(F32)) * scale).T
    over.wait_send()
    for k in range(2):
        for axis in range(2):
            for copy in first[k][axis][3] + second[k][axis][3]:
                copy.wait_send()


def project_call(full, yt, w_out, qkv, c, scale):
    feats = full.shape[1]
    width = w_out.shape[1]
    tokens = qkv.shape[1]
    vm = pl.BlockSpec(memory_space=pltpu.VMEM)
    hb = pl.BlockSpec(memory_space=pl.ANY)
    return pl.pallas_call(
        functools.partial(project_kernel, scale),
        out_shape=(
            jax.ShapeDtypeStruct((feats // 32, width), F32),
            jax.ShapeDtypeStruct((tokens, width), BF16),
            jax.ShapeDtypeStruct((tokens, width), BF16),
        ),
        in_specs=[vm, vm, hb, hb, vm],
        out_specs=(vm, vm, vm),
        scratch_shapes=[
            pltpu.VMEM((feats, width), BF16),
            pltpu.VMEM((tokens, width), BF16),
            pltpu.VMEM((2, 4, 4, width, LANES), BF16),
            pltpu.VMEM((2, 2, 2, 4, 256, LANES), BF16),
            pltpu.VMEM((2, 2, 4, 4, 256, LANES), BF16),
            pltpu.VMEM((2, 2, 4, 512, LANES), BF16),
            pltpu.VMEM((2, 2, 2, 256, LANES), BF16),
            pltpu.VMEM((2, 2, 4, 256, LANES), BF16),
            pltpu.VMEM((width, LANES), BF16),
            pltpu.VMEM((width, LANES), F32),
            pltpu.VMEM((width, LANES), BF16),
            pltpu.SemaphoreType.DMA((2,)),
            pltpu.SemaphoreType.DMA((2, 2, 6)),
            pltpu.SemaphoreType.DMA((2, 2, 6)),
            pltpu.SemaphoreType.DMA((2, 2, 6)),
            pltpu.SemaphoreType.DMA((2, 2, 6)),
            pltpu.SemaphoreType.DMA,
            pltpu.SemaphoreType.DMA,
        ],
        compiler_params=pltpu.CompilerParams(
            vmem_limit_bytes=60 * 1024 * 1024, collective_id=0, has_side_effects=True
        ),
        name="project",
    )(full, yt, w_out, qkv, c)


def local(qkv, filters, w_out, cotangent, doc_lens):
    count = lax.axis_size("ctx")
    tokens = qkv.shape[1] * count
    scale = 1.0 / math.sqrt(tokens)
    conv, gated, win, full = conv_call(doc_lens, filters, qkv, cotangent, count)
    grad_w, grad_c, grad_q = project_call(full, gated, w_out, qkv, conv, scale)
    grad_qkv, taps = back_call(doc_lens, filters, qkv, win, grad_c, grad_q, count)
    return grad_qkv, jnp.flip(taps, axis=1) * scale, grad_w


def solution(mesh):
    return jax.shard_map(
        local,
        mesh=mesh,
        in_specs=(P(None, "ctx", "tp"), P("tp", None), P(None, "tp"), P(("ctx", "tp"), None), P()),
        out_specs=(P(None, "ctx", "tp"), P("tp", None), P("ctx", "tp")),
        check_vma=False,
    )
```
